32 devices in a mesh: sec: 4 (over y, x), dom: 8 (over z, core).
Axes of the slice: x: 2, y: 2, z: 4, core: 2. Of those that a mesh axis runs over, the one named last changes fastest.
Arguments:
- state_init: float32 [4, 8, 6, 1536], P('sec', 'dom'), may hold values from -6 to 6
- right_side: float32 [4, 8, 6, 1536], P('sec', 'dom'), may hold values from -6 to 6
- diag_inverse: float32 [4, 8, 6, 6, 1536], P('sec', 'dom'), may hold values from -1.2 to 2, as said below
- face_block: bfloat16 [4, 8, 6, 6, 9216], P('sec', 'dom'), may hold values from -0.47851562 to 0.47851562
- face_target: int32 [4, 8, 9216], P('sec', 'dom'), may hold values from 0 to 1535
- face_source: int32 [4, 8, 9216], P('sec', 'dom'), may hold values from 0 to 3071, as said below
- face_count: int32 [4, 8], P('sec', 'dom'), may hold values from 4608 to 9216, as said below
- send_list: int32 [4, 8, 1536], P('sec', 'dom'), may hold values from 0 to 1535
- surf_cell: int32 [4, 8, 128], P('sec', 'dom'), may hold values from 0 to 1535
- surf_count: int32 [4, 8, 8], P('sec', 'dom'), may hold values from 0 to 16, as said below
- surf_map: float32 [4, 8, 3, 6, 128], P('sec', 'dom'), may hold values from -3 to 3
- surf_node: int32 [3, 8, 128], P(None, 'dom'), may hold values from 0 to 1535
Outputs:
- state_final: float32 [4, 8, 6, 1536], P('sec', 'dom')
The draws below stay inside these ranges and needn't reach their ends.
Inputs may be any that keep to these rules, and one draw needn't show every extreme that they name: `face_source`: values below 1536 name the partition's own cells; a value 1536 + r * 192 + k names slot k of neighbour block r, which comes from partition d - offset r of the same section; only existing partitions are read, and each block is read in a leading run of its slots whose length differs from block to block; some block's run is 192 long. Only the first face_count entries of a partition's face lists are live; some partition lists 9216 live entries. Live slots of a flow partition towards structure partition o are its first surf_count slots of that block. Only some flow partitions (those at the wall, drawn from the seed) have live slots, each towards a few structure partitions of consecutive index (mod 8); some pair has 16 live slots. The structure section's row is zero and not read. `diag_inverse`: each block is a transposed block inverse; its diagonal entries are positive.
All inputs are finite; a program needn't handle non-finite values.
Results may differ from the reference program's by a relative error of at most 0.0003.
Values sent between devices are 32-bit elements; how exact they have to be, the bound alone decides.
A program may use at most 128 MiB of HBM per device.

```python
import jax
import jax.numpy as jnp
from jax import lax

NVAR = 6
NLOAD = 3
NBR = 8
CELLS = 1536
HCAP = 192
CAP = 16
ITERS = 2
FACES = 9216
GHOSTS = 1536
SLOTS = 128
N_SEC = 4
N_DOM = 8


neighbour_offsets = (1, -1, 2, -2, 3, -3, 4, -4)


def neighbour_counts(key):
    subkeys = jax.random.split(jax.random.fold_in(key, 20), 2)
    dims = (N_SEC, N_DOM, NBR)
    counts = jax.random.randint(subkeys[0], dims, 1, HCAP + 1)
    offsets = jnp.array(neighbour_offsets, dtype=jnp.int32)
    senders = jnp.arange(N_DOM, dtype=jnp.int32)[None, :, None] - offsets[None, None, :]
    exists = (senders >= 0) & (senders < N_DOM)
    fullest = jax.random.randint(subkeys[1], (), 1, N_DOM)
    forced = (jnp.arange(N_DOM, dtype=jnp.int32)[None, :, None] == fullest) & (jnp.arange(NBR, dtype=jnp.int32)[None, None, :] == 0)
    counts = jnp.where(forced, HCAP, counts)
    return jnp.where(exists, counts, 0).astype(jnp.int32)


def draw_face_source(key, part):
    counts = neighbour_counts(key)
    subkeys = jax.random.split(jax.random.fold_in(key, 11), 4)
    dims = (N_SEC, N_DOM, FACES)
    local_cells = jax.random.randint(subkeys[0], dims, 0, CELLS)
    block = jax.random.randint(subkeys[1], dims, 0, NBR)
    block_count = jnp.take_along_axis(counts, block, axis=2)
    slot = jax.random.randint(subkeys[2], dims, 0, 1048576) % jnp.maximum(block_count, 1)
    ghost_cells = CELLS + block * HCAP + slot
    chooser = jax.random.randint(subkeys[3], dims, 0, 6)
    return jnp.where((chooser == 0) & (block_count > 0), ghost_cells, local_cells).astype(jnp.int32)


def draw_face_count(key, part):
    subkeys = jax.random.split(jax.random.fold_in(key, 12), 2)
    initial = jax.random.randint(subkeys[0], (N_SEC, N_DOM), FACES // 2, FACES + 1)
    fullest = jax.random.randint(subkeys[1], (), 0, N_SEC * N_DOM)
    flat_index = jnp.arange(N_SEC * N_DOM, dtype=jnp.int32).reshape(N_SEC, N_DOM)
    return jnp.where(flat_index == fullest, FACES, initial).astype(jnp.int32)


def draw_surf_count(key, part):
    subkeys = jax.random.split(jax.random.fold_in(key, 13), 7)
    dims = (N_SEC, N_DOM, N_DOM)
    initial = jax.random.randint(subkeys[0], dims, 1, CAP + 1)
    at_wall = jax.random.randint(subkeys[1], (N_SEC, N_DOM), 0, 4) == 0
    first_owner = jax.random.randint(subkeys[2], (N_SEC, N_DOM), 0, N_DOM)
    reach = jax.random.randint(subkeys[3], (N_SEC, N_DOM), 2, 5)
    owners = jnp.arange(N_DOM, dtype=jnp.int32)[None, None, :]
    coupled = (owners - first_owner[:, :, None]) % N_DOM < reach[:, :, None]
    pick_sec = jax.random.randint(subkeys[4], (), 0, N_SEC - 1)
    pick_dom = jax.random.randint(subkeys[5], (), 0, N_DOM)
    sec_ids = jnp.arange(N_SEC, dtype=jnp.int32)[:, None]
    dom_ids = jnp.arange(N_DOM, dtype=jnp.int32)[None, :]
    chosen = (sec_ids == pick_sec) & (dom_ids == pick_dom)
    at_wall = at_wall | chosen
    forced = chosen[:, :, None] & (owners == first_owner[:, :, None])
    counts = jnp.where(forced, CAP, initial)
    flow_rows = (jnp.arange(N_SEC, dtype=jnp.int32) < N_SEC - 1)[:, None, None]
    live = at_wall[:, :, None] & coupled & flow_rows
    return jnp.where(live, counts, 0).astype(jnp.int32)


def draw_diag_inverse(key, part):
    subkeys = jax.random.split(jax.random.fold_in(key, 14), 2)
    scales = jnp.exp(jax.random.uniform(subkeys[0], (N_SEC, N_DOM, NVAR, CELLS), jnp.float32, jnp.log(0.2), jnp.log(2.0)))
    noise = jnp.clip(jax.random.normal(subkeys[1], (N_SEC, N_DOM, NVAR, NVAR, CELLS), jnp.float32), -3.0, 3.0)
    roots = jnp.sqrt(scales)
    outer = roots[:, :, :, None, :] * roots[:, :, None, :, :]
    identity = (jnp.arange(NVAR)[:, None] == jnp.arange(NVAR)[None, :]).astype(jnp.float32)[None, None, :, :, None]
    diagonal = scales[:, :, :, None, :] * identity
    return (diagonal + (1.0 - identity) * 0.2 * outer * noise).astype(jnp.float32)


def place_ends(values, stream_key, low, top_value):
    shape = values.shape
    index_at = [jax.random.randint(jax.random.fold_in(stream_key, axis), (), 0, shape[axis]) for axis in range(len(shape))]
    values = values.at[tuple(index_at)].set(low)
    longest = shape.index(max(shape))
    index_at[longest] = (index_at[longest] + 1) % shape[longest]
    return values.at[tuple(index_at)].set(top_value)


def level_of(rng, shape, cuts, low, high):
    factor_of = 1.0
    for axis_at, blocks in cuts:
        heights = jax.random.uniform(jax.random.fold_in(jax.random.fold_in(rng, 6), axis_at), (blocks,), jnp.float32, low / len(cuts), high / len(cuts))
        factor_of = factor_of * jnp.repeat(jnp.exp(heights), shape[axis_at] // blocks).reshape((-1,) + (1,) * (len(shape) - 1 - axis_at))
    return factor_of


def gaussian(own_key, shape, scale, limit, cuts=(), kind=jnp.bfloat16):
    result = jax.random.normal(own_key, shape, jnp.float32) * scale
    if len(cuts) > 0:
        result = level_of(own_key, shape, cuts, -0.22, 0.18) * result
    return jnp.clip(result, min=-limit, max=limit).astype(kind)


def setup_inputs(seed: int = 0) -> dict:
    streams_of = jax.random.split(jax.random.key(seed), 13)
    state_init = gaussian(streams_of[0], (N_SEC, N_DOM, NVAR, CELLS), 1.0, 6.0, ((0, 4), (1, 8)), jnp.float32)
    right_side = gaussian(streams_of[1], (N_SEC, N_DOM, NVAR, CELLS), 1.0, 6.0, ((0, 4), (1, 8)), jnp.float32)
    diag_inverse = draw_diag_inverse(jax.random.fold_in(streams_of[12], 71), 0)
    face_block = gaussian(streams_of[3], (N_SEC, N_DOM, NVAR, NVAR, FACES), 0.08, 0.47851562, ((0, 4), (1, 8)))
    face_target = place_ends(jax.random.randint(streams_of[4], (N_SEC, N_DOM, FACES), 0, CELLS), jax.random.fold_in(streams_of[4], 1), 0, CELLS - 1).astype(jnp.int32)
    face_source = draw_face_source(jax.random.fold_in(streams_of[12], 71), 0)
    face_count = draw_face_count(jax.random.fold_in(streams_of[12], 71), 0)
    send_list = place_ends(jax.random.randint(streams_of[7], (N_SEC, N_DOM, GHOSTS), 0, CELLS), jax.random.fold_in(streams_of[7], 1), 0, CELLS - 1).astype(jnp.int32)
    surf_cell = place_ends(jax.random.randint(streams_of[8], (N_SEC, N_DOM, SLOTS), 0, CELLS), jax.random.fold_in(streams_of[8], 1), 0, CELLS - 1).astype(jnp.int32)
    surf_count = draw_surf_count(jax.random.fold_in(streams_of[12], 71), 0)
    surf_map = gaussian(streams_of[10], (N_SEC, N_DOM, NLOAD, NVAR, SLOTS), 0.5, 3.0, ((0, 4), (1, 8)), jnp.float32)
    surf_node = place_ends(jax.random.randint(streams_of[11], (N_SEC - 1, N_DOM, SLOTS), 0, CELLS), jax.random.fold_in(streams_of[11], 1), 0, CELLS - 1).astype(jnp.int32)
    return dict(state_init=state_init, right_side=right_side, diag_inverse=diag_inverse, face_block=face_block, face_target=face_target, face_source=face_source, face_count=face_count, send_list=send_list, surf_cell=surf_cell, surf_count=surf_count, surf_map=surf_map, surf_node=surf_node)


neighbour_offsets = (1, -1, 2, -2, 3, -3, 4, -4)


def apply_blocks(blocks, vector):
    width = blocks.shape[-2]
    total = blocks[..., :, 0, :].astype(jnp.float32) * vector[..., 0:1, :]
    for column in range(1, width):
        total = total + blocks[..., :, column, :].astype(jnp.float32) * vector[..., column:column + 1, :]
    return total


def apply_transposed(blocks, vector):
    height = blocks.shape[-3]
    total = blocks[..., 0, :, :].astype(jnp.float32) * vector[..., 0:1, :]
    for row_index in range(1, height):
        total = total + blocks[..., row_index, :, :].astype(jnp.float32) * vector[..., row_index:row_index + 1, :]
    return total


def take_columns(matrix, indices):
    return matrix[:, indices]


select_nested = jax.vmap(jax.vmap(take_columns))


def scatter_columns(values, indices):
    return jnp.zeros((values.shape[0], CELLS), jnp.float32).at[:, indices].add(values)


scatter_nested = jax.vmap(jax.vmap(scatter_columns))


def face_sum(packed):
    extended, blocks, targets, sources, live_mask = packed
    gathered = extended[:, sources]
    contrib = apply_blocks(blocks, gathered) * live_mask[None, :]
    return jnp.zeros((NVAR, CELLS), jnp.float32).at[:, targets].add(contrib)


def load_into(node_ids, values):
    flat_ids = node_ids.reshape(-1)
    flat_values = jnp.transpose(values, (1, 0, 2)).reshape(NLOAD, -1)
    return jnp.zeros((NLOAD, CELLS), jnp.float32).at[:, flat_ids].add(flat_values)


def shift_partitions(piece, offset):
    blank = jnp.zeros((piece.shape[0], abs(offset)) + piece.shape[2:], jnp.float32)
    if offset > 0:
        return jnp.concatenate([blank, piece[:, :N_DOM - offset]], axis=1)
    return jnp.concatenate([piece[:, -offset:], blank], axis=1)


def reference(state_init, right_side, diag_inverse, face_block, face_target, face_source, face_count, send_list, surf_cell, surf_count, surf_map, surf_node):
    final_row = N_SEC - 1
    ghost_total = NBR * HCAP
    slot_total = N_DOM * CAP
    face_live = (jnp.arange(FACES, dtype=jnp.int32)[None, None, :] < face_count[:, :, None]).astype(jnp.float32)
    slot_live = (jnp.arange(CAP, dtype=jnp.int32)[None, None, None, :] < surf_count[:, :, :, None]).astype(jnp.float32)
    flow_flag = (jnp.arange(N_SEC, dtype=jnp.int32) < final_row).astype(jnp.float32)
    slot_live = slot_live.reshape(N_SEC, N_DOM, slot_total) * flow_flag[:, None, None]
    partitions = N_SEC * N_DOM
    state = state_init
    for sweep in range(ITERS):
        outgoing = select_nested(state, send_list).reshape(N_SEC, N_DOM, NVAR, NBR, HCAP)
        received = [shift_partitions(outgoing[:, :, :, index, :], neighbour_offsets[index]) for index in range(NBR)]
        ghosts = jnp.stack(received, axis=3).reshape(N_SEC, N_DOM, NVAR, ghost_total)
        extended = jnp.concatenate([state, ghosts], axis=3)
        face_terms = lax.map(face_sum, (
            extended.reshape(partitions, NVAR, CELLS + ghost_total),
            face_block.reshape(partitions, NVAR, NVAR, FACES),
            face_target.reshape(partitions, FACES),
            face_source.reshape(partitions, FACES),
            face_live.reshape(partitions, FACES))).reshape(N_SEC, N_DOM, NVAR, CELLS)
        loads = apply_blocks(surf_map, select_nested(state, surf_cell)) * slot_live[:, :, None, :]
        arrived = loads[:final_row].reshape(final_row, N_DOM, NLOAD, N_DOM, CAP)
        arrived = jnp.transpose(arrived, (0, 3, 2, 1, 4)).reshape(final_row, N_DOM, NLOAD, slot_total)
        load_total = jax.vmap(load_into, in_axes=(1, 1))(surf_node, arrived)
        struct_disp = state[final_row, :, :NLOAD, :]
        looked = jax.vmap(jax.vmap(take_columns, in_axes=(None, 0)), in_axes=(0, 1), out_axes=1)(struct_disp, surf_node)
        returned = looked.reshape(final_row, N_DOM, NLOAD, N_DOM, CAP)
        returned = jnp.transpose(returned, (0, 3, 2, 1, 4)).reshape(final_row, N_DOM, NLOAD, slot_total)
        returned = returned * slot_live[:final_row, :, None, :]
        pushed = apply_transposed(surf_map[:final_row], returned)
        flow_coupling = scatter_nested(pushed, surf_cell[:final_row])
        struct_coupling = jnp.concatenate([load_total, jnp.zeros((N_DOM, NVAR - NLOAD, CELLS), jnp.float32)], axis=1)
        coupling = jnp.concatenate([flow_coupling, struct_coupling[None]], axis=0)
        state = apply_blocks(diag_inverse, right_side - face_terms - coupling)
    return state
```

```python
import functools

import jax
import jax.numpy as jnp
from jax import lax
from jax.experimental import pallas as pl
from jax.experimental.pallas import tpu as pltpu
from jax.sharding import PartitionSpec as P

NVAR = 6
NLOAD = 3
NBR = 8
ITERS = 2
LANES = 128
LANE_BITS = 7
ROWS = 8
LOW = 256
CHUNK = 1024

neighbour_offsets = (1, -1, 2, -2, 3, -3, 4, -4)

F32 = jnp.float32
BF16 = jnp.bfloat16


def lane_gather(table, index):
    return jnp.take_along_axis(table, index, axis=1, mode="promise_in_bounds")


def spread(row):
    return jnp.broadcast_to(row, (ROWS, row.shape[-1]))


def gather_tiles(tiles, high, low):
    found = [lane_gather(tile, low) for tile in tiles]
    bit = 1
    while len(found) > 1:
        odd = (high & bit) != 0
        pairs = [found[at : at + 2] for at in range(0, len(found), 2)]
        found = [jnp.where(odd, pair[1], pair[0]) if len(pair) == 2 else pair[0] for pair in pairs]
        bit *= 2
    return found[0]


def split_index(index):
    index = spread(index)
    return index >> LANE_BITS, index & (LANES - 1)


def sum_rows(parts):
    width = parts[0].shape[1]
    row = lax.broadcasted_iota(jnp.int32, (ROWS, width), 0)
    parts = list(parts) + [None] * (ROWS - len(parts))
    step = ROWS // 2
    while step >= 1:
        upper = (row & step) == 0
        merged = []
        for at in range(step):
            a, b = parts[at], parts[at + step]
            if a is None and b is None:
                merged.append(None)
                continue
            if b is None:
                kept, moved = jnp.where(upper, a, 0.0), jnp.where(upper, 0.0, a)
            else:
                kept, moved = jnp.where(upper, a, b), jnp.where(upper, b, a)
            if step == ROWS // 2:
                moved = pltpu.roll(moved, step, 0)
            else:
                moved = jnp.where(upper, pltpu.roll(moved, ROWS - step, 0), pltpu.roll(moved, step, 0))
            merged.append(kept + moved)
        parts = merged
        step //= 2
    return parts[0]


def pad_rows(value):
    return jnp.concatenate([value, jnp.zeros((ROWS - value.shape[0], value.shape[1]), value.dtype)], axis=0)


def kernel(
    dims,
    state_init,
    right_side,
    inverse,
    face_block,
    face_target,
    face_source,
    face_count,
    send_list,
    surf_cell,
    surf_count,
    surf_map,
    surf_node,
    out_ref,
    init_v,
    right_v,
    inverse_v,
    block_v,
    target_v,
    source_v,
    count_s,
    list_v,
    cell_v,
    live_s,
    map_v,
    node_v,
    state_buf,
    out_buf,
    halo_recv,
    ghost_buf,
    gath,
    diagonal,
    onehot,
    target_high,
    load_send,
    load_recv,
    disp_send,
    disp_recv,
    halo_send_sem,
    halo_recv_sem,
    surf_send_sem,
    load_recv_sem,
    disp_recv_sem,
    fetch_sem,
):
    n_sec, n_dom, cells, faces, slots, ghosts = dims
    flow = n_sec - 1
    tiles = cells // LANES
    ghost_tiles = ghosts // LANES
    block_slots = ghosts // NBR
    surf_tiles = slots // LANES
    cap = slots // n_dom
    per_tile = LANES // cap
    highs = cells // LOW
    sec = lax.axis_index("sec")
    dom = lax.axis_index("dom")
    is_structure = sec == flow
    lane = lax.broadcasted_iota(jnp.int32, (ROWS, LANES), 1)
    lane_block = lane // cap

    def present(offset):
        target = dom + offset
        return (target >= 0) & (target < n_dom)

    order = (
        (state_init, init_v),
        (send_list, list_v),
        (surf_node, node_v),
        (surf_cell, cell_v),
        (surf_map, map_v),
        (surf_count, live_s),
        (face_block, block_v),
        (face_target, target_v),
        (face_source, source_v),
        (face_count, count_s),
        (right_side, right_v),
        (inverse, inverse_v),
    )
    fetches = [pltpu.make_async_copy(src, dst, fetch_sem.at[at]) for at, (src, dst) in enumerate(order)]
    for fetch in fetches:
        fetch.start()

    halo_recv[...] = jnp.zeros(halo_recv.shape, F32)
    load_recv[...] = jnp.zeros(load_recv.shape, F32)
    disp_recv[...] = jnp.zeros(disp_recv.shape, F32)

    barrier = pltpu.get_barrier_semaphore()
    partners = jnp.where(is_structure, flow * n_dom, n_dom)
    for offset in neighbour_offsets:
        partners = partners + present(offset).astype(jnp.int32)

        @pl.when(present(offset))
        def _():
            pl.semaphore_signal(barrier, inc=1, device_id={"dom": dom + offset})

    @pl.when(is_structure)
    def _():
        @pl.loop(0, flow * n_dom)
        def _(at):
            pl.semaphore_signal(barrier, inc=1, device_id={"sec": at // n_dom, "dom": at % n_dom})

    @pl.when(jnp.logical_not(is_structure))
    def _():
        @pl.loop(0, n_dom)
        def _(at):
            pl.semaphore_signal(barrier, inc=1, device_id={"sec": flow, "dom": at})

    def piece_tiles(index):
        start, end = index * block_slots, (index + 1) * block_slots
        return start, end, start // LANES, (end + LANES - 1) // LANES

    def halo_copy(sweep, index):
        _, _, first, last = piece_tiles(index)
        width = (last - first) * LANES
        return pltpu.make_async_remote_copy(
            src_ref=out_buf.at[sweep, :, pl.ds(first * LANES, width)],
            dst_ref=halo_recv.at[sweep, index, :, pl.ds(0, width)],
            send_sem=halo_send_sem.at[sweep, index],
            recv_sem=halo_recv_sem.at[sweep, index],
            device_id={"dom": dom + neighbour_offsets[index]},
        )

    sub = lax.broadcasted_iota(jnp.int32, (ROWS, LANES), 0)
    block_lane = sub * cap + lane % cap

    def pack(values):
        packed = jnp.zeros((ROWS, LANES), F32)
        for row in range(NLOAD):
            packed = jnp.where(lane_block == row, lane_gather(spread(values[row : row + 1]), block_lane), packed)
        return packed

    def unpack(rows):
        values = jnp.zeros((ROWS, LANES), F32)
        for part, row in enumerate(rows):
            values = jnp.where(lane_block == part, lane_gather(spread(row), block_lane), values)
        return values

    def two_terms(values):
        first = values.astype(BF16)
        second = (values - first.astype(F32)).astype(BF16)
        return jnp.concatenate([first, second], axis=0)

    def live_mask(tile):
        limit = jnp.zeros((ROWS, LANES), jnp.int32)
        for part in range(per_tile):
            limit = jnp.where(lane_block == part, live_s[0, 0, tile * per_tile + part], limit)
        return (lane % cap) < limit

    def state_tiles():
        return [state_buf[:, at * LANES : (at + 1) * LANES] for at in range(tiles)]

    def prepare(sweep):
        own = state_tiles()
        for at in range(ghost_tiles):
            columns = slice(at * LANES, (at + 1) * LANES)
            out_buf[sweep, :, columns] = gather_tiles(own, *split_index(list_v[0, :, columns]))

    def map_rows(row, tile):
        return map_v[row * NVAR : (row + 1) * NVAR, 0, tile * LANES : (tile + 1) * LANES]

    def prepare_surface(sweep):
        own = state_tiles()

        @pl.when(is_structure)
        def _():
            for section in range(flow):
                for tile in range(surf_tiles):
                    index = node_v[section, :, tile * LANES : (tile + 1) * LANES]
                    packed = pack(gather_tiles(own, *split_index(index)))
                    for part in range(per_tile):
                        disp_send[sweep, section * n_dom + tile * per_tile + part] = packed[part : part + 1]

        @pl.when(jnp.logical_not(is_structure))
        def _():
            for tile in range(surf_tiles):
                index = cell_v[0, :, tile * LANES : (tile + 1) * LANES]
                values = gather_tiles(own, *split_index(index))
                loads = sum_rows([pad_rows(map_rows(row, tile) * values[:NVAR]) for row in range(NLOAD)])
                packed = pack(jnp.where(live_mask(tile), loads, 0.0))
                for part in range(per_tile):
                    load_send[sweep, tile * per_tile + part] = packed[part : part + 1]

    def send_halo(sweep):
        for index in range(NBR):

            @pl.when(present(neighbour_offsets[index]))
            def _():
                halo_copy(sweep, index).start()

    def send_surface(sweep):
        @pl.when(is_structure)
        def _():
            @pl.loop(0, flow * n_dom)
            def _(at):
                section, part = at // n_dom, at % n_dom
                pltpu.make_async_remote_copy(
                    src_ref=disp_send.at[sweep, at],
                    dst_ref=disp_recv.at[sweep, dom],
                    send_sem=surf_send_sem.at[sweep],
                    recv_sem=disp_recv_sem.at[sweep],
                    device_id={"sec": section, "dom": part},
                ).start()

        @pl.when(jnp.logical_not(is_structure))
        def _():
            @pl.loop(0, n_dom)
            def _(at):
                pltpu.make_async_remote_copy(
                    src_ref=load_send.at[sweep, at],
                    dst_ref=load_recv.at[sweep, sec * n_dom + dom],
                    send_sem=surf_send_sem.at[sweep],
                    recv_sem=load_recv_sem.at[sweep],
                    device_id={"sec": flow, "dom": at},
                ).start()

    def one_hot(low, rows):
        row = lax.broadcasted_iota(jnp.int32, (rows, low.shape[1]), 0)
        return jnp.where(row == low, 1.0, 0.0).astype(BF16)

    def build_diagonals():
        bits = [(sub & (1 << bit)) != 0 for bit in range(3)]

        @pl.loop(0, faces // LANES)
        def _(at):
            part = pl.ds(pl.multiple_of(at * LANES, LANES), LANES)
            found = [pad_rows(block_v[0, 0, row, :, part].astype(F32)) for row in range(NVAR)]
            found = found + [jnp.zeros((ROWS, LANES), F32)] * (ROWS - NVAR)
            for bit in range(3):
                found = [jnp.where(bits[bit], found[(at + (1 << bit)) % ROWS], found[at]) for at in range(ROWS)]
            for shift in range(ROWS):
                diagonal[shift, :, part] = found[(ROWS - shift) % ROWS]

    def build_targets():
        row = lax.broadcasted_iota(jnp.int32, (LOW, LANES), 0).astype(F32).astype(BF16)
        one, zero = jnp.ones((LOW, LANES), BF16), jnp.zeros((LOW, LANES), BF16)
        live = count_s[0, 0]
        entry = lax.broadcasted_iota(jnp.int32, (1, LANES), 1)

        @pl.loop(0, faces // LANES)
        def _(at):
            part = pl.ds(pl.multiple_of(at * LANES, LANES), LANES)
            cell = target_v[0, :, part]
            low = jnp.broadcast_to((cell & (LOW - 1)).astype(F32), (LOW, LANES)).astype(BF16)
            onehot[:, part] = jnp.where(row == low, one, zero)
            high = jnp.where(entry + at * LANES < live, cell // LOW, highs)
            target_high[:, part] = jnp.broadcast_to(high.astype(F32), (2 * ROWS, LANES)).astype(BF16)

    def local_gather():
        own = state_tiles()

        @pl.loop(0, faces // CHUNK)
        def _(at):
            for piece in range(CHUNK // LANES):
                part = pl.ds(pl.multiple_of(at * CHUNK + piece * LANES, LANES), LANES)
                gath[:, part] = gather_tiles(own, *split_index(source_v[0, :, part]))

    def receive_halo(sweep):
        for index in range(NBR):

            @pl.when(present(-neighbour_offsets[index]))
            def _():
                halo_copy(sweep, index).wait_recv()

        for at in range(ghost_tiles):
            total = jnp.zeros((ROWS, LANES), F32)
            for index in range(NBR):
                start, end, first, last = piece_tiles(index)
                if first <= at < last:
                    inside = (lane + at * LANES >= start) & (lane + at * LANES < end)
                    part = halo_recv[sweep, index, :, (at - first) * LANES : (at - first + 1) * LANES]
                    total = jnp.where(inside, part, total)
            ghost_buf[:, at * LANES : (at + 1) * LANES] = total

    def spread_highs(both, high):
        return jnp.concatenate([jnp.where(high == at, both, jnp.zeros_like(both)) for at in range(highs)], axis=0)

    def masked_dot(values, high, rhs):
        both = two_terms(values)
        high = jnp.broadcast_to(high.astype(F32), both.shape).astype(BF16)
        lhs = spread_highs(both, high)
        return lax.dot_general(lhs, rhs, (((1,), (1,)), ((), ())), preferred_element_type=F32)

    def turn(value, by):
        return pltpu.roll(value, (ROWS - by) % ROWS, 0)

    def face_pass():
        halo = [ghost_buf[:, at * LANES : (at + 1) * LANES] for at in range(ghost_tiles)]

        def step(at, total):
            base = at * CHUNK
            pieces = []
            for piece in range(CHUNK // LANES):
                part = pl.ds(pl.multiple_of(base + piece * LANES, LANES), LANES)
                high, low = split_index(source_v[0, :, part])
                high = high - tiles
                value = jnp.where(high >= 0, gather_tiles(halo, high, low), gath[:, part])
                terms = [diagonal[shift, :, part] * value for shift in range(ROWS)]
                terms = [terms[shift] + turn(terms[shift + 4], 4) for shift in range(4)]
                contrib = terms[0] + turn(terms[1], 1) + turn(terms[2] + turn(terms[3], 1), 2)
                pieces.append(spread_highs(two_terms(contrib), target_high[:, part]))
            lhs = jnp.concatenate(pieces, axis=1)
            columns = pl.ds(pl.multiple_of(base, CHUNK), CHUNK)
            return total + lax.dot_general(
                lhs, onehot[:, columns], (((1,), (1,)), ((), ())), preferred_element_type=F32
            )

        return lax.fori_loop(0, faces // CHUNK, step, jnp.zeros((2 * ROWS * highs, LOW), F32))

    def surface_pass(sweep):
        @pl.when(is_structure)
        def _():
            pltpu.make_async_copy(load_recv.at[sweep], load_recv.at[sweep], load_recv_sem.at[sweep]).wait()

        @pl.when(jnp.logical_not(is_structure))
        def _():
            pltpu.make_async_copy(disp_recv.at[sweep], disp_recv.at[sweep], disp_recv_sem.at[sweep]).wait()

        total = None
        for section in range(flow):
            for tile in range(surf_tiles):
                columns = slice(tile * LANES, (tile + 1) * LANES)
                first = section * n_dom + tile * per_tile
                values = unpack([load_recv[sweep, first + part] for part in range(per_tile)])
                cell = node_v[section, :, columns]
                if section == 0:
                    back = unpack([disp_recv[sweep, tile * per_tile + part] for part in range(per_tile)])
                    back = jnp.where(live_mask(tile), back, 0.0)
                    pushed = map_rows(0, tile) * back[0:1]
                    for row in range(1, NLOAD):
                        pushed = pushed + map_rows(row, tile) * back[row : row + 1]
                    values = jnp.where(is_structure, values, pad_rows(pushed))
                    cell = jnp.where(is_structure, cell, cell_v[0, :, columns])
                else:
                    values = jnp.where(is_structure, values, 0.0)
                term = masked_dot(values, cell // LOW, one_hot(cell % LOW, LOW))
                total = term if total is None else total + term
        return total

    fetches[0].wait()
    for at in range(tiles):
        state_buf[:, at * LANES : (at + 1) * LANES] = pad_rows(init_v[pl.ds(at, NVAR, stride=tiles), :])
    fetches[1].wait()
    prepare(0)
    for fetch in fetches[2:6]:
        fetch.wait()
    prepare_surface(0)
    fetches[6].wait()
    build_diagonals()
    fetches[7].wait()
    fetches[9].wait()
    build_targets()
    pl.semaphore_wait(barrier, partners)
    send_halo(0)
    send_surface(0)
    fetches[8].wait()
    for fetch in fetches[10:]:
        fetch.wait()
    for sweep in range(ITERS):
        if sweep > 0:
            prepare(sweep)
            send_halo(sweep)
            prepare_surface(sweep)
            send_surface(sweep)
        local_gather()
        receive_halo(sweep)
        total = face_pass()
        total = total + surface_pass(sweep)
        for at in range(tiles):
            base = 2 * ROWS * (at * LANES // LOW)
            columns = slice(at * LANES % LOW, at * LANES % LOW + LANES)
            gone = total[base : base + ROWS, columns] + total[base + ROWS : base + 2 * ROWS, columns]
            rest = right_v[pl.ds(at, NVAR, stride=tiles), :] - gone[:NVAR]
            fresh = sum_rows(
                [
                    pad_rows(inverse_v[pl.ds(row * NVAR * tiles + at, NVAR, stride=tiles), :] * rest)
                    for row in range(NVAR)
                ]
            )
            if sweep == ITERS - 1:
                out_ref[pl.ds(at, NVAR, stride=tiles), :] = fresh[:NVAR]
            else:
                state_buf[:, at * LANES : (at + 1) * LANES] = fresh

    for sweep in range(ITERS):
        for index in range(NBR):

            @pl.when(present(neighbour_offsets[index]))
            def _():
                halo_copy(sweep, index).wait_send()

        @pl.when(is_structure)
        def _():
            pltpu.make_async_copy(load_recv.at[sweep], load_recv.at[sweep], surf_send_sem.at[sweep]).wait()

        @pl.when(jnp.logical_not(is_structure))
        def _():
            pltpu.make_async_copy(disp_recv.at[sweep], disp_recv.at[sweep], surf_send_sem.at[sweep]).wait()


def body(n_sec, n_dom, *args):
    cells = args[0].shape[-1]
    faces = args[4].shape[-1]
    ghosts = args[7].shape[-1]
    slots = args[8].shape[-1]
    flow = n_sec - 1
    piece = (2 * LANES - 1 + ghosts // NBR) // LANES * LANES
    args = list(args)
    for at in (0, 1, 2):
        args[at] = args[at].reshape(-1, LANES)
    args[10] = args[10].reshape(NLOAD * NVAR, 1, slots)
    fetched = [pltpu.VMEM(value.shape, value.dtype) for value in args]
    for at in (6, 9):
        fetched[at] = pltpu.SMEM(args[at].shape, args[at].dtype)
    out = pl.pallas_call(
        functools.partial(kernel, (n_sec, n_dom, cells, faces, slots, ghosts)),
        out_shape=jax.ShapeDtypeStruct(args[0].shape, F32),
        in_specs=[pl.BlockSpec(memory_space=pltpu.HBM)] * len(args),
        out_specs=pl.BlockSpec(memory_space=pltpu.VMEM),
        scratch_shapes=[
            *fetched,
            pltpu.VMEM((ROWS, cells), F32),
            pltpu.VMEM((ITERS, ROWS, ghosts), F32),
            pltpu.VMEM((ITERS, NBR, ROWS, piece), F32),
            pltpu.VMEM((ROWS, ghosts), F32),
            pltpu.VMEM((ROWS, faces), F32),
            pltpu.VMEM((ROWS, ROWS, faces), F32),
            pltpu.VMEM((LOW, faces), BF16),
            pltpu.VMEM((2 * ROWS, faces), BF16),
            pltpu.VMEM((ITERS, n_dom, 1, LANES), F32),
            pltpu.VMEM((ITERS, flow * n_dom, 1, LANES), F32),
            pltpu.VMEM((ITERS, flow * n_dom, 1, LANES), F32),
            pltpu.VMEM((ITERS, n_dom, 1, LANES), F32),
            pltpu.SemaphoreType.DMA((ITERS, NBR)),
            pltpu.SemaphoreType.DMA((ITERS, NBR)),
            pltpu.SemaphoreType.DMA((ITERS,)),
            pltpu.SemaphoreType.DMA((ITERS,)),
            pltpu.SemaphoreType.DMA((ITERS,)),
            pltpu.SemaphoreType.DMA((len(args),)),
        ],
        compiler_params=pltpu.CompilerParams(
            collective_id=0, has_side_effects=True, vmem_limit_bytes=63 * 1024 * 1024 + 768 * 1024
        ),
    )(*args)
    return out.reshape(1, 1, NVAR, cells)


def solution(mesh):
    in_specs = (
        P("sec", "dom", None, None),
        P("sec", "dom", None, None),
        P("sec", "dom", None, None, None),
        P("sec", "dom", None, None, None),
        P("sec", "dom", None),
        P("sec", "dom", None),
        P("sec", "dom"),
        P("sec", "dom", None),
        P("sec", "dom", None),
        P("sec", "dom", None),
        P("sec", "dom", None, None, None),
        P(None, "dom", None),
    )
    out_specs = P("sec", "dom", None, None)
    run = functools.partial(body, mesh.shape["sec"], mesh.shape["dom"])
    return jax.shard_map(run, mesh=mesh, in_specs=in_specs, out_specs=out_specs, check_vma=False)
```

```python
import functools

import jax
import jax.numpy as jnp
from jax import lax
from jax.experimental import pallas as pl
from jax.experimental.pallas import tpu as pltpu
from jax.sharding import PartitionSpec as P

NVAR = 6
NLOAD = 3
NBR = 8
ITERS = 2
LANES = 128
LANE_BITS = 7
ROWS = 8
LOW = 256
CHUNK = 3072
STEP = 8

neighbour_offsets = (1, -1, 2, -2, 3, -3, 4, -4)

F32 = jnp.float32
BF16 = jnp.bfloat16


def lane_gather(table, index):
    return jnp.take_along_axis(table, index, axis=1, mode="promise_in_bounds")


def spread(row):
    return jnp.broadcast_to(row, (ROWS, row.shape[-1]))


def gather_tiles(tiles, high, low):
    found = [lane_gather(tile, low) for tile in tiles]
    bit = 1
    while len(found) > 1:
        odd = (high & bit) != 0
        pairs = [found[at : at + 2] for at in range(0, len(found), 2)]
        found = [jnp.where(odd, pair[1], pair[0]) if len(pair) == 2 else pair[0] for pair in pairs]
        bit *= 2
    return found[0]


def split_index(index):
    index = spread(index)
    return index >> LANE_BITS, index & (LANES - 1)


def sum_rows(parts):
    width = parts[0].shape[1]
    row = lax.broadcasted_iota(jnp.int32, (ROWS, width), 0)
    parts = list(parts) + [None] * (ROWS - len(parts))
    step = ROWS // 2
    while step >= 1:
        upper = (row & step) == 0
        merged = []
        for at in range(step):
            a, b = parts[at], parts[at + step]
            if a is None and b is None:
                merged.append(None)
                continue
            if b is None:
                kept, moved = jnp.where(upper, a, 0.0), jnp.where(upper, 0.0, a)
            else:
                kept, moved = jnp.where(upper, a, b), jnp.where(upper, b, a)
            if step == ROWS // 2:
                moved = pltpu.roll(moved, step, 0)
            else:
                moved = jnp.where(upper, pltpu.roll(moved, ROWS - step, 0), pltpu.roll(moved, step, 0))
            merged.append(kept + moved)
        parts = merged
        step //= 2
    return parts[0]


def pad_rows(value):
    return jnp.concatenate([value, jnp.zeros((ROWS - value.shape[0], value.shape[1]), value.dtype)], axis=0)


def kernel(
    dims,
    state_init,
    right_side,
    inverse,
    face_block,
    face_target,
    face_source,
    count_s,
    send_list,
    surf_cell,
    surf_count,
    surf_map,
    surf_node,
    out_ref,
    init_v,
    right_v,
    inverse_v,
    block_v,
    target_v,
    source_v,
    list_v,
    cell_v,
    live_s,
    map_v,
    node_v,
    state_buf,
    out_buf,
    halo_recv,
    ghost_buf,
    gath,
    diagonal,
    inverse_diagonal,
    right_rows,
    onehot,
    target_high,
    surf_hot,
    surf_high,
    surf_total,
    load_send,
    load_recv,
    disp_send,
    disp_recv,
    halo_send_sem,
    halo_recv_sem,
    surf_send_sem,
    load_recv_sem,
    disp_recv_sem,
    fetch_sem,
    ready_sem,
):
    n_sec, n_dom, cells, faces, slots, ghosts = dims
    flow = n_sec - 1
    tiles = cells // LANES
    ghost_tiles = ghosts // LANES
    block_slots = ghosts // NBR
    surf_tiles = slots // LANES
    cap = slots // n_dom
    per_tile = LANES // cap
    highs = cells // LOW
    sec = lax.axis_index("sec")
    dom = lax.axis_index("dom")
    is_structure = sec == flow
    lane = lax.broadcasted_iota(jnp.int32, (ROWS, LANES), 1)
    lane_block = lane // cap

    def present(offset):
        target = dom + offset
        return (target >= 0) & (target < n_dom)

    order = (
        (state_init, init_v),
        (send_list, list_v),
        (surf_node, node_v),
        (surf_cell, cell_v),
        (surf_map, map_v),
        (surf_count, live_s),
        (face_block, block_v),
        (face_target, target_v),
        (face_source, source_v),
        (right_side, right_v),
        (inverse, inverse_v),
    )
    fetches = [pltpu.make_async_copy(src, dst, fetch_sem.at[at]) for at, (src, dst) in enumerate(order)]
    for fetch in fetches:
        fetch.start()

    halo_recv[...] = jnp.zeros(halo_recv.shape, F32)
    load_recv[...] = jnp.zeros(load_recv.shape, F32)
    disp_recv[...] = jnp.zeros(disp_recv.shape, F32)

    barrier = pltpu.get_barrier_semaphore()
    partners = jnp.where(is_structure, flow * n_dom, 0)
    for offset in neighbour_offsets:
        partners = partners + present(offset).astype(jnp.int32)

        @pl.when(present(offset))
        def _():
            pl.semaphore_signal(barrier, inc=1, device_id={"dom": dom + offset})

    @pl.when(jnp.logical_not(is_structure))
    def _():
        @pl.loop(0, n_dom)
        def _(at):
            pl.semaphore_signal(barrier, inc=1, device_id={"sec": flow, "dom": at})

    def greet_flow():
        @pl.loop(0, flow * n_dom)
        def _(at):
            pl.semaphore_signal(ready_sem, inc=1, device_id={"sec": at // n_dom, "dom": at % n_dom})

    def piece_tiles(index):
        start, end = index * block_slots, (index + 1) * block_slots
        return start, end, start // LANES, (end + LANES - 1) // LANES

    def halo_copy(sweep, index):
        _, _, first, last = piece_tiles(index)
        width = (last - first) * LANES
        return pltpu.make_async_remote_copy(
            src_ref=out_buf.at[sweep, pl.ds(0, NVAR), pl.ds(first * LANES, width)],
            dst_ref=halo_recv.at[sweep, index, pl.ds(0, NVAR), pl.ds(0, width)],
            send_sem=halo_send_sem.at[sweep, index],
            recv_sem=halo_recv_sem.at[sweep, index],
            device_id={"dom": dom + neighbour_offsets[index]},
        )

    sub = lax.broadcasted_iota(jnp.int32, (ROWS, LANES), 0)
    block_lane = sub * cap + lane % cap

    def pack(values):
        packed = jnp.zeros((ROWS, LANES), F32)
        for row in range(NLOAD):
            packed = jnp.where(lane_block == row, lane_gather(spread(values[row : row + 1]), block_lane), packed)
        return packed

    def unpack(rows):
        values = jnp.zeros((ROWS, LANES), F32)
        for part, row in enumerate(rows):
            values = jnp.where(lane_block == part, lane_gather(spread(row), block_lane), values)
        return values

    def split_highs(values, high):
        first = values.astype(BF16).astype(F32)
        second = values - first
        rows = []
        for at in range(highs):
            here = high == at
            rows += [jnp.where(here, first, 0.0), jnp.where(here, second, 0.0)]
        return jnp.concatenate(rows, axis=0).astype(BF16)

    def scatter(lhs, rhs):
        return lax.dot_general(lhs, rhs, (((1,), (1,)), ((), ())), preferred_element_type=F32)

    def live_mask(tile):
        limit = jnp.zeros((ROWS, LANES), jnp.int32)
        for part in range(per_tile):
            limit = jnp.where(lane_block == part, live_s[0, 0, tile * per_tile + part], limit)
        return (lane % cap) < limit

    def state_tiles():
        return [state_buf[:, at * LANES : (at + 1) * LANES] for at in range(tiles)]

    def prepare(sweep):
        own = state_tiles()
        for at in range(ghost_tiles):
            columns = slice(at * LANES, (at + 1) * LANES)
            out_buf[sweep, :, columns] = gather_tiles(own, *split_index(list_v[0, :, columns]))

    def map_rows(row, tile):
        return map_v[row * NVAR : (row + 1) * NVAR, 0, tile * LANES : (tile + 1) * LANES]

    def prepare_disp(sweep):
        own = state_tiles()
        for section in range(flow):
            for tile in range(surf_tiles):
                index = node_v[section, :, tile * LANES : (tile + 1) * LANES]
                packed = pack(gather_tiles(own, *split_index(index)))
                for part in range(per_tile):
                    disp_send[sweep, section * n_dom + tile * per_tile + part] = packed[part : part + 1]

    def prepare_loads(sweep):
        own = state_tiles()
        for tile in range(surf_tiles):
            index = cell_v[0, :, tile * LANES : (tile + 1) * LANES]
            values = gather_tiles(own, *split_index(index))
            loads = sum_rows([pad_rows(map_rows(row, tile) * values[:NVAR]) for row in range(NLOAD)])
            packed = pack(jnp.where(live_mask(tile), loads, 0.0))
            for part in range(per_tile):
                load_send[sweep, tile * per_tile + part] = packed[part : part + 1]

    def send_halo(sweep):
        for index in range(NBR):

            @pl.when(present(neighbour_offsets[index]))
            def _():
                halo_copy(sweep, index).start()

    def send_disp(sweep):
        @pl.loop(0, flow * n_dom)
        def _(at):
            section, part = at // n_dom, at % n_dom
            pltpu.make_async_remote_copy(
                src_ref=disp_send.at[sweep, at],
                dst_ref=disp_recv.at[sweep, dom],
                send_sem=surf_send_sem.at[sweep],
                recv_sem=disp_recv_sem.at[sweep],
                device_id={"sec": section, "dom": part},
            ).start()

    def send_loads(sweep):
        @pl.loop(0, n_dom)
        def _(at):
            pltpu.make_async_remote_copy(
                src_ref=load_send.at[sweep, at],
                dst_ref=load_recv.at[sweep, sec * n_dom + dom],
                send_sem=surf_send_sem.at[sweep],
                recv_sem=load_recv_sem.at[sweep],
                device_id={"sec": flow, "dom": at},
            ).start()

    bits = [(sub & (1 << bit)) != 0 for bit in range(3)]

    def by_diagonals(found):
        found = [pad_rows(value) for value in found] + [jnp.zeros((ROWS, LANES), F32)] * (ROWS - NVAR)
        for bit in range(3):
            found = [jnp.where(bits[bit], found[(at + (1 << bit)) % ROWS], found[at]) for at in range(ROWS)]
        return [found[(ROWS - shift) % ROWS] for shift in range(ROWS)]

    def turn(value, by):
        return pltpu.roll(value, (ROWS - by) % ROWS, 0)

    def apply_diagonals(diagonals, value):
        terms = [diagonals[shift] * value for shift in range(ROWS)]
        terms = [terms[shift] + turn(terms[shift + 4], 4) for shift in range(4)]
        return terms[0] + turn(terms[1], 1) + turn(terms[2] + turn(terms[3], 1), 2)

    low_row = lax.broadcasted_iota(jnp.int32, (LOW, LANES), 0).astype(F32).astype(BF16)
    ones, zeros = jnp.ones((LOW, LANES), BF16), jnp.zeros((LOW, LANES), BF16)

    def one_hot(cell):
        low = jnp.broadcast_to((cell & (LOW - 1)).astype(F32), (LOW, LANES)).astype(BF16)
        return jnp.where(low_row == low, ones, zeros)

    def build_faces():
        live = count_s[0, 0]
        entry = lax.broadcasted_iota(jnp.int32, (1, LANES), 1)

        @pl.loop(0, faces // (STEP * LANES))
        def _(at):
            for piece in range(STEP):
                group = at * STEP + piece
                part = pl.ds(pl.multiple_of(group * LANES, LANES), LANES)
                found = by_diagonals([block_v[0, 0, row, :, part].astype(F32) for row in range(NVAR)])
                for shift in range(ROWS):
                    diagonal[group, shift] = found[shift]
                cell = target_v[0, :, part]
                onehot[group] = one_hot(cell)
                target_high[group] = jnp.where(entry + group * LANES < live, cell // LOW, highs)

    def build_cells():
        for at in range(tiles):
            columns = slice(at * LANES, (at + 1) * LANES)
            right_rows[:, columns] = pad_rows(right_v[pl.ds(at, NVAR, stride=tiles), :])
            found = by_diagonals(
                [inverse_v[pl.ds(row * NVAR * tiles + at, NVAR, stride=tiles), :] for row in range(NVAR)]
            )
            for shift in range(ROWS):
                inverse_diagonal[at, shift] = found[shift]

    def build_surface():
        for section in range(flow):
            for tile in range(surf_tiles):
                columns = slice(tile * LANES, (tile + 1) * LANES)
                cell = node_v[section, :, columns]
                if section == 0:
                    cell = jnp.where(is_structure, cell, cell_v[0, :, columns])
                surf_hot[section * surf_tiles + tile] = one_hot(cell)
                surf_high[section * surf_tiles + tile] = cell // LOW

    def local_gather():
        own = state_tiles()

        @pl.loop(0, faces // CHUNK)
        def _(at):
            for piece in range(CHUNK // LANES):
                part = pl.ds(pl.multiple_of(at * CHUNK + piece * LANES, LANES), LANES)
                gath[:, part] = gather_tiles(own, *split_index(source_v[0, :, part]))

    def receive_halo(sweep):
        for index in range(NBR):

            @pl.when(present(-neighbour_offsets[index]))
            def _():
                halo_copy(sweep, index).wait_recv()

        for at in range(ghost_tiles):
            total = jnp.zeros((ROWS, LANES), F32)
            for index in range(NBR):
                start, end, first, last = piece_tiles(index)
                if first <= at < last:
                    inside = (lane + at * LANES >= start) & (lane + at * LANES < end)
                    part = halo_recv[sweep, index, :, (at - first) * LANES : (at - first + 1) * LANES]
                    total = jnp.where(inside, part, total)
            ghost_buf[:, at * LANES : (at + 1) * LANES] = total

    def face_pass():
        halo = [ghost_buf[:, at * LANES : (at + 1) * LANES] for at in range(ghost_tiles)]

        def step(at, total):
            lhs, rhs = [], []
            for piece in range(CHUNK // LANES):
                group = at * (CHUNK // LANES) + piece
                part = pl.ds(pl.multiple_of(group * LANES, LANES), LANES)
                high, low = split_index(source_v[0, :, part])
                high = high - tiles
                value = jnp.where(high >= 0, gather_tiles(halo, high, low), gath[:, part])
                contrib = apply_diagonals([diagonal[group, shift] for shift in range(ROWS)], value)
                lhs.append(split_highs(contrib, spread(target_high[group])))
                rhs.append(onehot[group])
            return total + scatter(jnp.concatenate(lhs, axis=1), jnp.concatenate(rhs, axis=1))

        return lax.fori_loop(0, faces // CHUNK, step, jnp.zeros((2 * ROWS * highs, LOW), F32))

    def surface_pass(sweep):
        @pl.when(is_structure)
        def _():
            pltpu.make_async_copy(load_recv.at[sweep], load_recv.at[sweep], load_recv_sem.at[sweep]).wait()
            lhs, rhs = [], []
            for section in range(flow):
                for tile in range(surf_tiles):
                    first = section * n_dom + tile * per_tile
                    at = section * surf_tiles + tile
                    values = unpack([load_recv[sweep, first + part] for part in range(per_tile)])
                    lhs.append(split_highs(values, spread(surf_high[at])))
                    rhs.append(surf_hot[at])
            surf_total[...] = scatter(jnp.concatenate(lhs, axis=1), jnp.concatenate(rhs, axis=1))

        @pl.when(jnp.logical_not(is_structure))
        def _():
            pltpu.make_async_copy(disp_recv.at[sweep], disp_recv.at[sweep], disp_recv_sem.at[sweep]).wait()
            lhs, rhs = [], []
            for tile in range(surf_tiles):
                back = unpack([disp_recv[sweep, tile * per_tile + part] for part in range(per_tile)])
                back = jnp.where(live_mask(tile), back, 0.0)
                pushed = map_rows(0, tile) * back[0:1]
                for row in range(1, NLOAD):
                    pushed = pushed + map_rows(row, tile) * back[row : row + 1]
                lhs.append(split_highs(pad_rows(pushed), spread(surf_high[tile])))
                rhs.append(surf_hot[tile])
            surf_total[...] = scatter(jnp.concatenate(lhs, axis=1), jnp.concatenate(rhs, axis=1))

    fetches[0].wait()
    for at in range(tiles):
        state_buf[:, at * LANES : (at + 1) * LANES] = pad_rows(init_v[pl.ds(at, NVAR, stride=tiles), :])
    fetches[1].wait()
    prepare(0)
    pl.semaphore_wait(barrier, partners)
    send_halo(0)
    for fetch in fetches[2:6]:
        fetch.wait()

    @pl.when(is_structure)
    def _():
        greet_flow()
        prepare_disp(0)
        send_disp(0)

    @pl.when(jnp.logical_not(is_structure))
    def _():
        prepare_loads(0)

    build_surface()
    for fetch in fetches[6:8]:
        fetch.wait()
    build_faces()
    for fetch in fetches[8:]:
        fetch.wait()
    build_cells()
    local_gather()

    @pl.when(jnp.logical_not(is_structure))
    def _():
        pl.semaphore_wait(ready_sem, n_dom)
        send_loads(0)

    for sweep in range(ITERS):
        if sweep > 0:

            @pl.when(is_structure)
            def _():
                prepare_disp(sweep)
                send_disp(sweep)

            prepare(sweep)
            send_halo(sweep)

            @pl.when(jnp.logical_not(is_structure))
            def _():
                prepare_loads(sweep)
                send_loads(sweep)

            local_gather()
        receive_halo(sweep)
        total = face_pass()
        surface_pass(sweep)
        total = total + surf_total[...]
        for at in range(tiles):
            base = 2 * ROWS * (at * LANES // LOW)
            columns = slice(at * LANES % LOW, at * LANES % LOW + LANES)
            gone = total[base : base + ROWS, columns] + total[base + ROWS : base + 2 * ROWS, columns]
            rest = right_rows[:, at * LANES : (at + 1) * LANES] - gone
            fresh = apply_diagonals([inverse_diagonal[at, shift] for shift in range(ROWS)], rest)
            if sweep == ITERS - 1:
                out_ref[pl.ds(at, NVAR, stride=tiles), :] = fresh[:NVAR]
            else:
                state_buf[:, at * LANES : (at + 1) * LANES] = fresh

    for sweep in range(ITERS):
        for index in range(NBR):

            @pl.when(present(neighbour_offsets[index]))
            def _():
                halo_copy(sweep, index).wait_send()

        @pl.when(is_structure)
        def _():
            pltpu.make_async_copy(load_recv.at[sweep], load_recv.at[sweep], surf_send_sem.at[sweep]).wait()

        @pl.when(jnp.logical_not(is_structure))
        def _():
            pltpu.make_async_copy(disp_recv.at[sweep], disp_recv.at[sweep], surf_send_sem.at[sweep]).wait()


def body(n_sec, n_dom, *args):
    cells = args[0].shape[-1]
    faces = args[4].shape[-1]
    ghosts = args[7].shape[-1]
    slots = args[8].shape[-1]
    flow = n_sec - 1
    piece = (2 * LANES - 1 + ghosts // NBR) // LANES * LANES
    args = list(args)
    for at in (0, 1, 2):
        args[at] = args[at].reshape(-1, LANES)
    args[10] = args[10].reshape(NLOAD * NVAR, 1, slots)
    fetched = [pltpu.VMEM(value.shape, value.dtype) for value in args]
    fetched[9] = pltpu.SMEM(args[9].shape, args[9].dtype)
    del fetched[6]
    groups = faces // LANES
    flat_rows = args[0].shape
    args = [value if at == 6 else pltpu.with_memory_space_constraint(value, pltpu.HBM) for at, value in enumerate(args)]
    specs = [pl.BlockSpec(memory_space=pltpu.HBM)] * len(args)
    specs[6] = pl.BlockSpec(memory_space=pltpu.SMEM)
    out = pl.pallas_call(
        functools.partial(kernel, (n_sec, n_dom, cells, faces, slots, ghosts)),
        out_shape=pltpu.VMEM(flat_rows, F32),
        in_specs=specs,
        out_specs=pl.BlockSpec(memory_space=pltpu.VMEM),
        scratch_shapes=[
            *fetched,
            pltpu.VMEM((ROWS, cells), F32),
            pltpu.VMEM((ITERS, ROWS, ghosts), F32),
            pltpu.VMEM((ITERS, NBR, ROWS, piece), F32),
            pltpu.VMEM((ROWS, ghosts), F32),
            pltpu.VMEM((ROWS, faces), F32),
            pltpu.VMEM((groups, ROWS, ROWS, LANES), F32),
            pltpu.VMEM((cells // LANES, ROWS, ROWS, LANES), F32),
            pltpu.VMEM((ROWS, cells), F32),
            pltpu.VMEM((groups, LOW, LANES), BF16),
            pltpu.VMEM((groups, 1, LANES), jnp.int32),
            pltpu.VMEM((flow * slots // LANES, LOW, LANES), BF16),
            pltpu.VMEM((flow * slots // LANES, 1, LANES), jnp.int32),
            pltpu.VMEM((2 * ROWS * (cells // LOW), LOW), F32),
            pltpu.VMEM((ITERS, n_dom, 1, LANES), F32),
            pltpu.VMEM((ITERS, flow * n_dom, 1, LANES), F32),
            pltpu.VMEM((ITERS, flow * n_dom, 1, LANES), F32),
            pltpu.VMEM((ITERS, n_dom, 1, LANES), F32),
            pltpu.SemaphoreType.DMA((ITERS, NBR)),
            pltpu.SemaphoreType.DMA((ITERS, NBR)),
            pltpu.SemaphoreType.DMA((ITERS,)),
            pltpu.SemaphoreType.DMA((ITERS,)),
            pltpu.SemaphoreType.DMA((ITERS,)),
            pltpu.SemaphoreType.DMA((len(fetched),)),
            pltpu.SemaphoreType.REGULAR,
        ],
        compiler_params=pltpu.CompilerParams(
            collective_id=0, has_side_effects=True, vmem_limit_bytes=48 * 1024 * 1024
        ),
    )(*args)
    return out.reshape(1, 1, NVAR, cells)


def solution(mesh):
    in_specs = (
        P("sec", "dom", None, None),
        P("sec", "dom", None, None),
        P("sec", "dom", None, None, None),
        P("sec", "dom", None, None, None),
        P("sec", "dom", None),
        P("sec", "dom", None),
        P("sec", "dom"),
        P("sec", "dom", None),
        P("sec", "dom", None),
        P("sec", "dom", None),
        P("sec", "dom", None, None, None),
        P(None, "dom", None),
    )
    out_specs = P("sec", "dom", None, None)
    run = functools.partial(body, mesh.shape["sec"], mesh.shape["dom"])
    return jax.shard_map(run, mesh=mesh, in_specs=in_specs, out_specs=out_specs, check_vma=False)
```

```python
import functools

import jax
import jax.numpy as jnp
from jax import lax
from jax.experimental import pallas as pl
from jax.experimental.pallas import tpu as pltpu
from jax.sharding import PartitionSpec as P

NVAR = 6
NLOAD = 3
NBR = 8
ITERS = 2
LANES = 128
LANE_BITS = 7
ROWS = 8
LOW = 128
CHUNK = 4608
STEP = 8
REACH = 4
FAR = 6

neighbour_offsets = (1, -1, 2, -2, 3, -3, 4, -4)

F32 = jnp.float32
BF16 = jnp.bfloat16


def lane_gather(table, index):
    return jnp.take_along_axis(table, index, axis=1, mode="promise_in_bounds")


def spread(row):
    return jnp.broadcast_to(row, (ROWS, row.shape[-1]))


def gather_tiles(tiles, high, low):
    found = [lane_gather(tile, low) for tile in tiles]
    bit = 1
    while len(found) > 1:
        odd = (high & bit) != 0
        pairs = [found[at : at + 2] for at in range(0, len(found), 2)]
        found = [jnp.where(odd, pair[1], pair[0]) if len(pair) == 2 else pair[0] for pair in pairs]
        bit *= 2
    return found[0]


def split_index(index):
    index = spread(index)
    return index >> LANE_BITS, index & (LANES - 1)


def sum_rows(parts):
    width = parts[0].shape[1]
    row = lax.broadcasted_iota(jnp.int32, (ROWS, width), 0)
    parts = list(parts) + [None] * (ROWS - len(parts))
    step = ROWS // 2
    while step >= 1:
        upper = (row & step) == 0
        merged = []
        for at in range(step):
            a, b = parts[at], parts[at + step]
            if a is None and b is None:
                merged.append(None)
                continue
            if b is None:
                kept, moved = jnp.where(upper, a, 0.0), jnp.where(upper, 0.0, a)
            else:
                kept, moved = jnp.where(upper, a, b), jnp.where(upper, b, a)
            if step == ROWS // 2:
                moved = pltpu.roll(moved, step, 0)
            else:
                moved = jnp.where(upper, pltpu.roll(moved, ROWS - step, 0), pltpu.roll(moved, step, 0))
            merged.append(kept + moved)
        parts = merged
        step //= 2
    return parts[0]


def pad_rows(value):
    return jnp.concatenate([value, jnp.zeros((ROWS - value.shape[0], value.shape[1]), value.dtype)], axis=0)


def kernel(
    dims,
    state_init,
    right_side,
    inverse,
    face_block,
    face_target,
    face_source,
    count_s,
    send_list,
    surf_cell,
    surf_count,
    surf_map,
    surf_node,
    out_ref,
    init_v,
    right_v,
    inverse_v,
    block_v,
    target_v,
    source_v,
    list_v,
    cell_v,
    live_s,
    map_v,
    node_v,
    state_buf,
    out_buf,
    halo_recv,
    ghost_buf,
    gath,
    diagonal,
    inverse_diagonal,
    right_rows,
    onehot,
    target_high,
    surf_hot,
    surf_high,
    surf_total,
    load_send,
    load_recv,
    relay_recv,
    disp_send,
    disp_recv,
    halo_send_sem,
    halo_recv_sem,
    surf_send_sem,
    load_recv_sem,
    disp_recv_sem,
    fetch_sem,
    relay_send_sem,
    relay_recv_sem,
    surf_ready,
):
    n_sec, n_dom, cells, faces, slots, ghosts = dims
    flow = n_sec - 1
    tiles = cells // LANES
    ghost_tiles = ghosts // LANES
    block_slots = ghosts // NBR
    surf_tiles = slots // LANES
    cap = slots // n_dom
    per_tile = LANES // cap
    highs = cells // LOW
    sec = lax.axis_index("sec")
    dom = lax.axis_index("dom")
    is_structure = sec == flow
    lane = lax.broadcasted_iota(jnp.int32, (ROWS, LANES), 1)
    lane_block = lane // cap

    def present(offset):
        target = dom + offset
        return (target >= 0) & (target < n_dom)

    order = (
        (state_init, init_v),
        (send_list, list_v),
        (surf_node, node_v),
        (surf_cell, cell_v),
        (surf_map, map_v),
        (surf_count, live_s),
        (face_block, block_v),
        (face_target, target_v),
        (face_source, source_v),
        (right_side, right_v),
        (inverse, inverse_v),
    )
    fetches = [pltpu.make_async_copy(src, dst, fetch_sem.at[at]) for at, (src, dst) in enumerate(order)]
    for fetch in fetches:
        fetch.start()

    halo_recv[...] = jnp.zeros(halo_recv.shape, F32)
    load_recv[...] = jnp.zeros(load_recv.shape, F32)
    disp_recv[...] = jnp.zeros(disp_recv.shape, F32)

    barrier = pltpu.get_barrier_semaphore()
    chip = dom // 2 * 2
    known = jnp.minimum(chip + 2, n_dom)
    last = is_structure & (dom >= n_dom - 2)

    def far_owners(part):
        return jnp.minimum(part // 2 * 2 + FAR, n_dom)

    own_far = far_owners(dom)
    passed_far = jnp.where(dom >= REACH, far_owners(dom - REACH), n_dom)

    def column(first, last, act):
        @pl.loop(first, last)
        def _(part):
            for section in range(flow):
                act(section, part)

    partners = jnp.where(is_structure, flow * n_dom, known)
    for offset in neighbour_offsets:
        partners = partners + present(offset).astype(jnp.int32)

        @pl.when(present(offset))
        def _():
            pl.semaphore_signal(barrier, inc=1, device_id={"dom": dom + offset})

    @pl.when(is_structure)
    def _():
        def greet(section, part):
            pl.semaphore_signal(barrier, inc=1, device_id={"sec": section, "dom": part})

        column(chip, n_dom, greet)

    @pl.when(jnp.logical_not(is_structure))
    def _():
        @pl.loop(0, n_dom)
        def _(owner):
            pl.semaphore_signal(barrier, inc=1, device_id={"sec": flow, "dom": owner})

    def meet():
        pl.semaphore_wait(barrier, partners)

        @pl.when(is_structure)
        def _():
            def greet(section, part):
                pl.semaphore_signal(surf_ready.at[dom], inc=1, device_id={"sec": section, "dom": part})

            column(0, chip, greet)

    def piece_tiles(index):
        start, end = index * block_slots, (index + 1) * block_slots
        return start, end, start // LANES, (end + LANES - 1) // LANES

    def halo_copy(sweep, index):
        _, _, first, last = piece_tiles(index)
        width = (last - first) * LANES
        return pltpu.make_async_remote_copy(
            src_ref=out_buf.at[sweep, pl.ds(0, NVAR), pl.ds(first * LANES, width)],
            dst_ref=halo_recv.at[sweep, index, pl.ds(0, NVAR), pl.ds(0, width)],
            send_sem=halo_send_sem.at[sweep, index],
            recv_sem=halo_recv_sem.at[sweep, index],
            device_id={"dom": dom + neighbour_offsets[index]},
        )

    sub = lax.broadcasted_iota(jnp.int32, (ROWS, LANES), 0)
    block_lane = sub * cap + lane % cap

    def pack(values):
        packed = jnp.zeros((ROWS, LANES), F32)
        for row in range(NLOAD):
            packed = jnp.where(lane_block == row, lane_gather(spread(values[row : row + 1]), block_lane), packed)
        return packed

    def unpack(rows):
        values = jnp.zeros((ROWS, LANES), F32)
        for part, row in enumerate(rows):
            values = jnp.where(lane_block == part, lane_gather(spread(row), block_lane), values)
        return values

    def split_highs(values, high):
        first = values.astype(BF16).astype(F32)
        second = values - first
        rows = []
        for at in range(highs):
            here = high == at
            rows += [jnp.where(here, first, 0.0), jnp.where(here, second, 0.0)]
        return jnp.concatenate(rows, axis=0).astype(BF16)

    def scatter(lhs, rhs):
        return lax.dot_general(lhs, rhs, (((1,), (1,)), ((), ())), preferred_element_type=F32)

    def live_mask(tile):
        limit = jnp.zeros((ROWS, LANES), jnp.int32)
        for part in range(per_tile):
            limit = jnp.where(lane_block == part, live_s[0, 0, tile * per_tile + part], limit)
        return (lane % cap) < limit

    def state_tiles():
        return [state_buf[:, at * LANES : (at + 1) * LANES] for at in range(tiles)]

    def prepare(sweep):
        own = state_tiles()
        for at in range(ghost_tiles):
            columns = slice(at * LANES, (at + 1) * LANES)
            out_buf[sweep, :, columns] = gather_tiles(own, *split_index(list_v[0, :, columns]))

    def map_rows(row, tile):
        return map_v[row * NVAR : (row + 1) * NVAR, 0, tile * LANES : (tile + 1) * LANES]

    def prepare_disp(sweep):
        own = state_tiles()
        for section in range(flow):
            for tile in range(surf_tiles):
                index = node_v[section, :, tile * LANES : (tile + 1) * LANES]
                packed = pack(gather_tiles(own, *split_index(index)))
                for part in range(per_tile):
                    disp_send[sweep, section * n_dom + tile * per_tile + part] = packed[part : part + 1]

    def prepare_loads(sweep):
        own = state_tiles()
        for tile in range(surf_tiles):
            index = cell_v[0, :, tile * LANES : (tile + 1) * LANES]
            values = gather_tiles(own, *split_index(index))
            loads = sum_rows([pad_rows(map_rows(row, tile) * values[:NVAR]) for row in range(NLOAD)])
            packed = pack(jnp.where(live_mask(tile), loads, 0.0))
            for part in range(per_tile):
                load_send[sweep, tile * per_tile + part] = packed[part : part + 1]

    def send_halo(sweep):
        for index in range(NBR):

            @pl.when(present(neighbour_offsets[index]))
            def _():
                halo_copy(sweep, index).start()

    def send_disp(sweep):
        def send(section, part):
            pltpu.make_async_remote_copy(
                src_ref=disp_send.at[sweep, section * n_dom + part],
                dst_ref=disp_recv.at[sweep, dom],
                send_sem=surf_send_sem.at[sweep],
                recv_sem=disp_recv_sem.at[sweep],
                device_id={"sec": section, "dom": part},
            ).start()

        column(0, n_dom, send)

    def load_copy(sweep, owner):
        return pltpu.make_async_remote_copy(
            src_ref=load_send.at[sweep, owner],
            dst_ref=load_recv.at[sweep, sec * n_dom + dom],
            send_sem=surf_send_sem.at[sweep],
            recv_sem=load_recv_sem.at[sweep],
            device_id={"sec": flow, "dom": owner},
        )

    def send_loads(sweep, first, last):
        @pl.loop(first, last)
        def _(at):
            load_copy(sweep, first + last - 1 - at).start()

    def send_far_loads():
        @pl.loop(own_far, n_dom)
        def _(owner):
            pltpu.make_async_remote_copy(
                src_ref=load_send.at[0, owner],
                dst_ref=relay_recv.at[owner],
                send_sem=surf_send_sem.at[0],
                recv_sem=relay_recv_sem.at[owner],
                device_id={"dom": dom + REACH},
            ).start()

    def wait_relay(owner, sem):
        pltpu.make_async_copy(relay_recv.at[owner], relay_recv.at[owner], sem.at[owner]).wait()

    def send_late_loads():
        @pl.loop(known, n_dom)
        def _(at):
            owner = known + n_dom - 1 - at
            pl.semaphore_wait(surf_ready.at[owner], 1)

            @pl.when(owner < own_far)
            def _():
                load_copy(0, owner).start()

            @pl.when(owner >= passed_far)
            def _():
                wait_relay(owner, relay_recv_sem)
                pltpu.make_async_remote_copy(
                    src_ref=relay_recv.at[owner],
                    dst_ref=load_recv.at[0, sec * n_dom + dom - REACH],
                    send_sem=relay_send_sem.at[owner],
                    recv_sem=load_recv_sem.at[0],
                    device_id={"sec": flow, "dom": owner},
                ).start()

    bits = [(sub & (1 << bit)) != 0 for bit in range(3)]

    def by_diagonals(found):
        found = [pad_rows(value) for value in found] + [jnp.zeros((ROWS, LANES), F32)] * (ROWS - NVAR)
        for bit in range(3):
            found = [jnp.where(bits[bit], found[(at + (1 << bit)) % ROWS], found[at]) for at in range(ROWS)]
        return [found[(ROWS - shift) % ROWS] for shift in range(ROWS)]

    def turn(value, by):
        return pltpu.roll(value, (ROWS - by) % ROWS, 0)

    def apply_diagonals(diagonals, value):
        terms = [diagonals[shift] * value for shift in range(ROWS)]
        terms = [terms[shift] + turn(terms[shift + 4], 4) for shift in range(4)]
        return terms[0] + turn(terms[1], 1) + turn(terms[2] + turn(terms[3], 1), 2)

    low_row = lax.broadcasted_iota(jnp.int32, (LOW, LANES), 0).astype(F32).astype(BF16)
    ones, zeros = jnp.ones((LOW, LANES), BF16), jnp.zeros((LOW, LANES), BF16)

    def one_hot(cell):
        low = jnp.broadcast_to((cell & (LOW - 1)).astype(F32), (LOW, LANES)).astype(BF16)
        return jnp.where(low_row == low, ones, zeros)

    def build_faces():
        live = count_s[0, 0]
        entry = lax.broadcasted_iota(jnp.int32, (1, LANES), 1)

        @pl.loop(0, faces // (STEP * LANES))
        def _(at):
            for piece in range(STEP):
                group = at * STEP + piece
                part = pl.ds(pl.multiple_of(group * LANES, LANES), LANES)
                found = by_diagonals([block_v[0, 0, row, :, part].astype(F32) for row in range(NVAR)])
                for shift in range(ROWS):
                    diagonal[group, shift] = found[shift]
                cell = target_v[0, :, part]
                onehot[group] = one_hot(cell)
                target_high[group] = jnp.where(entry + group * LANES < live, cell // LOW, highs)

    def build_cells():
        for at in range(tiles):
            columns = slice(at * LANES, (at + 1) * LANES)
            right_rows[:, columns] = pad_rows(right_v[pl.ds(at, NVAR, stride=tiles), :])
            found = by_diagonals(
                [inverse_v[pl.ds(row * NVAR * tiles + at, NVAR, stride=tiles), :] for row in range(NVAR)]
            )
            for shift in range(ROWS):
                inverse_diagonal[at, shift] = found[shift]

    def build_surface():
        for section in range(flow):
            for tile in range(surf_tiles):
                columns = slice(tile * LANES, (tile + 1) * LANES)
                cell = node_v[section, :, columns]
                if section == 0:
                    cell = jnp.where(is_structure, cell, cell_v[0, :, columns])
                surf_hot[section * surf_tiles + tile] = one_hot(cell)
                surf_high[section * surf_tiles + tile] = cell // LOW

    def local_gather():
        own = state_tiles()

        @pl.loop(0, faces // CHUNK)
        def _(at):
            for piece in range(CHUNK // LANES):
                part = pl.ds(pl.multiple_of(at * CHUNK + piece * LANES, LANES), LANES)
                gath[:, part] = gather_tiles(own, *split_index(source_v[0, :, part]))

    def receive_halo(sweep):
        for index in range(NBR):

            @pl.when(present(-neighbour_offsets[index]))
            def _():
                halo_copy(sweep, index).wait_recv()

        for at in range(ghost_tiles):
            total = jnp.zeros((ROWS, LANES), F32)
            for index in range(NBR):
                start, end, first, last = piece_tiles(index)
                if first <= at < last:
                    inside = (lane + at * LANES >= start) & (lane + at * LANES < end)
                    part = halo_recv[sweep, index, :, (at - first) * LANES : (at - first + 1) * LANES]
                    total = jnp.where(inside, part, total)
            ghost_buf[:, at * LANES : (at + 1) * LANES] = total

    def face_pass():
        halo = [ghost_buf[:, at * LANES : (at + 1) * LANES] for at in range(ghost_tiles)]

        def step(at, total):
            lhs, rhs = [], []
            for piece in range(CHUNK // LANES):
                group = at * (CHUNK // LANES) + piece
                part = pl.ds(pl.multiple_of(group * LANES, LANES), LANES)
                high, low = split_index(source_v[0, :, part])
                high = high - tiles
                value = jnp.where(high >= 0, gather_tiles(halo, high, low), gath[:, part])
                contrib = apply_diagonals([diagonal[group, shift] for shift in range(ROWS)], value)
                lhs.append(split_highs(contrib, spread(target_high[group])))
                rhs.append(onehot[group])
            return total + scatter(jnp.concatenate(lhs, axis=1), jnp.concatenate(rhs, axis=1))

        return lax.fori_loop(0, faces // CHUNK, step, jnp.zeros((2 * ROWS * highs, LOW), F32))

    def surface_pass(sweep):
        @pl.when(is_structure)
        def _():
            pltpu.make_async_copy(load_recv.at[sweep], load_recv.at[sweep], load_recv_sem.at[sweep]).wait()
            lhs, rhs = [], []
            for section in range(flow):
                for tile in range(surf_tiles):
                    first = section * n_dom + tile * per_tile
                    at = section * surf_tiles + tile
                    values = unpack([load_recv[sweep, first + part] for part in range(per_tile)])
                    lhs.append(split_highs(values, spread(surf_high[at])))
                    rhs.append(surf_hot[at])
            surf_total[...] = scatter(jnp.concatenate(lhs, axis=1), jnp.concatenate(rhs, axis=1))

        @pl.when(jnp.logical_not(is_structure))
        def _():
            pltpu.make_async_copy(disp_recv.at[sweep], disp_recv.at[sweep], disp_recv_sem.at[sweep]).wait()
            lhs, rhs = [], []
            for tile in range(surf_tiles):
                back = unpack([disp_recv[sweep, tile * per_tile + part] for part in range(per_tile)])
                back = jnp.where(live_mask(tile), back, 0.0)
                pushed = map_rows(0, tile) * back[0:1]
                for row in range(1, NLOAD):
                    pushed = pushed + map_rows(row, tile) * back[row : row + 1]
                lhs.append(split_highs(pad_rows(pushed), spread(surf_high[tile])))
                rhs.append(surf_hot[tile])
            surf_total[...] = scatter(jnp.concatenate(lhs, axis=1), jnp.concatenate(rhs, axis=1))

    @pl.when(last)
    def _():
        meet()

    fetches[0].wait()
    for at in range(tiles):
        state_buf[:, at * LANES : (at + 1) * LANES] = pad_rows(init_v[pl.ds(at, NVAR, stride=tiles), :])
    fetches[1].wait()
    prepare(0)
    for fetch in fetches[2:6]:
        fetch.wait()

    @pl.when(is_structure)
    def _():
        prepare_disp(0)

    @pl.when(jnp.logical_not(is_structure))
    def _():
        prepare_loads(0)

    @pl.when(jnp.logical_not(last))
    def _():
        meet()

    send_halo(0)

    @pl.when(is_structure)
    def _():
        send_disp(0)

    @pl.when(jnp.logical_not(is_structure))
    def _():
        send_loads(0, 0, known)
        send_far_loads()

    build_surface()
    for fetch in fetches[6:8]:
        fetch.wait()
    build_faces()
    for fetch in fetches[8:]:
        fetch.wait()
    build_cells()
    local_gather()

    @pl.when(jnp.logical_not(is_structure))
    def _():
        send_late_loads()

    for sweep in range(ITERS):
        if sweep > 0:

            @pl.when(is_structure)
            def _():
                prepare_disp(sweep)
                send_disp(sweep)

            prepare(sweep)
            send_halo(sweep)

            @pl.when(jnp.logical_not(is_structure))
            def _():
                prepare_loads(sweep)
                send_loads(sweep, 0, n_dom)

            local_gather()
        receive_halo(sweep)
        total = face_pass()
        surface_pass(sweep)
        total = total + surf_total[...]
        for at in range(tiles):
            base = 2 * ROWS * (at * LANES // LOW)
            columns = slice(at * LANES % LOW, at * LANES % LOW + LANES)
            gone = total[base : base + ROWS, columns] + total[base + ROWS : base + 2 * ROWS, columns]
            rest = right_rows[:, at * LANES : (at + 1) * LANES] - gone
            fresh = apply_diagonals([inverse_diagonal[at, shift] for shift in range(ROWS)], rest)
            if sweep == ITERS - 1:
                out_ref[pl.ds(at, NVAR, stride=tiles), :] = fresh[:NVAR]
            else:
                state_buf[:, at * LANES : (at + 1) * LANES] = fresh

    for sweep in range(ITERS):
        for index in range(NBR):

            @pl.when(present(neighbour_offsets[index]))
            def _():
                halo_copy(sweep, index).wait_send()

        @pl.when(is_structure)
        def _():
            pltpu.make_async_copy(load_recv.at[sweep], load_recv.at[sweep], surf_send_sem.at[sweep]).wait()

        @pl.when(jnp.logical_not(is_structure))
        def _():
            pltpu.make_async_copy(disp_recv.at[sweep], disp_recv.at[sweep], surf_send_sem.at[sweep]).wait()

    @pl.when(jnp.logical_not(is_structure))
    def _():
        @pl.loop(passed_far, n_dom)
        def _(owner):
            wait_relay(owner, relay_send_sem)


def body(n_sec, n_dom, *args):
    cells = args[0].shape[-1]
    faces = args[4].shape[-1]
    ghosts = args[7].shape[-1]
    slots = args[8].shape[-1]
    flow = n_sec - 1
    piece = (2 * LANES - 1 + ghosts // NBR) // LANES * LANES
    args = list(args)
    for at in (0, 1, 2):
        args[at] = args[at].reshape(-1, LANES)
    args[10] = args[10].reshape(NLOAD * NVAR, 1, slots)
    fetched = [pltpu.VMEM(value.shape, value.dtype) for value in args]
    fetched[9] = pltpu.SMEM(args[9].shape, args[9].dtype)
    del fetched[6]
    groups = faces // LANES
    flat_rows = args[0].shape
    args = [value if at == 6 else pltpu.with_memory_space_constraint(value, pltpu.HBM) for at, value in enumerate(args)]
    specs = [pl.BlockSpec(memory_space=pltpu.HBM)] * len(args)
    specs[6] = pl.BlockSpec(memory_space=pltpu.SMEM)
    out = pl.pallas_call(
        functools.partial(kernel, (n_sec, n_dom, cells, faces, slots, ghosts)),
        out_shape=pltpu.VMEM(flat_rows, F32),
        in_specs=specs,
        out_specs=pl.BlockSpec(memory_space=pltpu.VMEM),
        scratch_shapes=[
            *fetched,
            pltpu.VMEM((ROWS, cells), F32),
            pltpu.VMEM((ITERS, ROWS, ghosts), F32),
            pltpu.VMEM((ITERS, NBR, ROWS, piece), F32),
            pltpu.VMEM((ROWS, ghosts), F32),
            pltpu.VMEM((ROWS, faces), F32),
            pltpu.VMEM((groups, ROWS, ROWS, LANES), F32),
            pltpu.VMEM((cells // LANES, ROWS, ROWS, LANES), F32),
            pltpu.VMEM((ROWS, cells), F32),
            pltpu.VMEM((groups, LOW, LANES), BF16),
            pltpu.VMEM((groups, 1, LANES), jnp.int32),
            pltpu.VMEM((flow * slots // LANES, LOW, LANES), BF16),
            pltpu.VMEM((flow * slots // LANES, 1, LANES), jnp.int32),
            pltpu.VMEM((2 * ROWS * (cells // LOW), LOW), F32),
            pltpu.VMEM((ITERS, n_dom, 1, LANES), F32),
            pltpu.VMEM((ITERS, flow * n_dom, 1, LANES), F32),
            pltpu.VMEM((n_dom, 1, LANES), F32),
            pltpu.VMEM((ITERS, flow * n_dom, 1, LANES), F32),
            pltpu.VMEM((ITERS, n_dom, 1, LANES), F32),
            pltpu.SemaphoreType.DMA((ITERS, NBR)),
            pltpu.SemaphoreType.DMA((ITERS, NBR)),
            pltpu.SemaphoreType.DMA((ITERS,)),
            pltpu.SemaphoreType.DMA((ITERS,)),
            pltpu.SemaphoreType.DMA((ITERS,)),
            pltpu.SemaphoreType.DMA((len(fetched),)),
            pltpu.SemaphoreType.DMA((n_dom,)),
            pltpu.SemaphoreType.DMA((n_dom,)),
            pltpu.SemaphoreType.REGULAR((n_dom,)),
        ],
        compiler_params=pltpu.CompilerParams(
            collective_id=0, has_side_effects=True, vmem_limit_bytes=48 * 1024 * 1024
        ),
    )(*args)
    return out.reshape(1, 1, NVAR, cells)


def solution(mesh):
    in_specs = (
        P("sec", "dom", None, None),
        P("sec", "dom", None, None),
        P("sec", "dom", None, None, None),
        P("sec", "dom", None, None, None),
        P("sec", "dom", None),
        P("sec", "dom", None),
        P("sec", "dom"),
        P("sec", "dom", None),
        P("sec", "dom", None),
        P("sec", "dom", None),
        P("sec", "dom", None, None, None),
        P(None, "dom", None),
    )
    out_specs = P("sec", "dom", None, None)
    run = functools.partial(body, mesh.shape["sec"], mesh.shape["dom"])
    return jax.shard_map(run, mesh=mesh, in_specs=in_specs, out_specs=out_specs, check_vma=False)
```

```python
import functools

import jax
import jax.numpy as jnp
from jax import lax
from jax.experimental import pallas as pl
from jax.experimental.pallas import tpu as pltpu
from jax.sharding import PartitionSpec as P

NVAR = 6
NLOAD = 3
NBR = 8
ITERS = 2
LANES = 128
LANE_BITS = 7
ROWS = 8
LOW = 128
CHUNK = 4608
STEP = 8
REACH = 4
FAR = 4

neighbour_offsets = (1, -1, 2, -2, 3, -3, 4, -4)

F32 = jnp.float32
BF16 = jnp.bfloat16


def lane_gather(table, index):
    return jnp.take_along_axis(table, index, axis=1, mode="promise_in_bounds")


def spread(row):
    return jnp.broadcast_to(row, (ROWS, row.shape[-1]))


def gather_tiles(tiles, high, low):
    found = [lane_gather(tile, low) for tile in tiles]
    bit = 1
    while len(found) > 1:
        odd = (high & bit) != 0
        pairs = [found[at : at + 2] for at in range(0, len(found), 2)]
        found = [jnp.where(odd, pair[1], pair[0]) if len(pair) == 2 else pair[0] for pair in pairs]
        bit *= 2
    return found[0]


def split_index(index):
    index = spread(index)
    return index >> LANE_BITS, index & (LANES - 1)


def sum_rows(parts):
    width = parts[0].shape[1]
    row = lax.broadcasted_iota(jnp.int32, (ROWS, width), 0)
    parts = list(parts) + [None] * (ROWS - len(parts))
    step = ROWS // 2
    while step >= 1:
        upper = (row & step) == 0
        merged = []
        for at in range(step):
            a, b = parts[at], parts[at + step]
            if a is None and b is None:
                merged.append(None)
                continue
            if b is None:
                kept, moved = jnp.where(upper, a, 0.0), jnp.where(upper, 0.0, a)
            else:
                kept, moved = jnp.where(upper, a, b), jnp.where(upper, b, a)
            if step == ROWS // 2:
                moved = pltpu.roll(moved, step, 0)
            else:
                moved = jnp.where(upper, pltpu.roll(moved, ROWS - step, 0), pltpu.roll(moved, step, 0))
            merged.append(kept + moved)
        parts = merged
        step //= 2
    return parts[0]


def pad_rows(value):
    return jnp.concatenate([value, jnp.zeros((ROWS - value.shape[0], value.shape[1]), value.dtype)], axis=0)


def kernel(
    dims,
    state_init,
    right_side,
    inverse,
    face_block,
    face_target,
    face_source,
    count_s,
    send_list,
    surf_cell,
    surf_count,
    surf_map,
    surf_node,
    out_ref,
    init_v,
    right_v,
    inverse_v,
    block_v,
    target_v,
    source_v,
    list_v,
    cell_v,
    live_s,
    map_v,
    node_v,
    state_buf,
    out_buf,
    halo_recv,
    ghost_buf,
    gath,
    diagonal,
    inverse_diagonal,
    right_rows,
    onehot,
    target_high,
    surf_hot,
    surf_high,
    surf_total,
    load_send,
    load_recv,
    relay_recv,
    disp_send,
    disp_recv,
    halo_send_sem,
    halo_recv_sem,
    surf_send_sem,
    load_recv_sem,
    disp_recv_sem,
    fetch_sem,
    relay_send_sem,
    relay_recv_sem,
    surf_ready,
):
    n_sec, n_dom, cells, faces, slots, ghosts = dims
    flow = n_sec - 1
    tiles = cells // LANES
    ghost_tiles = ghosts // LANES
    block_slots = ghosts // NBR
    surf_tiles = slots // LANES
    cap = slots // n_dom
    per_tile = LANES // cap
    highs = cells // LOW
    sec = lax.axis_index("sec")
    dom = lax.axis_index("dom")
    is_structure = sec == flow
    lane = lax.broadcasted_iota(jnp.int32, (ROWS, LANES), 1)
    lane_block = lane // cap

    def present(offset):
        target = dom + offset
        return (target >= 0) & (target < n_dom)

    order = (
        (state_init, init_v),
        (send_list, list_v),
        (surf_node, node_v),
        (surf_cell, cell_v),
        (surf_map, map_v),
        (surf_count, live_s),
        (face_block, block_v),
        (face_target, target_v),
        (face_source, source_v),
        (right_side, right_v),
        (inverse, inverse_v),
    )
    fetches = [pltpu.make_async_copy(src, dst, fetch_sem.at[at]) for at, (src, dst) in enumerate(order)]
    for fetch in fetches:
        fetch.start()

    halo_recv[...] = jnp.zeros(halo_recv.shape, F32)
    load_recv[...] = jnp.zeros(load_recv.shape, F32)
    disp_recv[...] = jnp.zeros(disp_recv.shape, F32)

    barrier = pltpu.get_barrier_semaphore()
    chip = dom // 2 * 2
    known = jnp.minimum(chip, n_dom)
    last = is_structure & (dom >= n_dom - 2)

    def far_owners(part):
        return jnp.minimum(part // 2 * 2 + FAR, n_dom)

    own_far = far_owners(dom)
    passed_far = jnp.where(dom >= REACH, far_owners(dom - REACH), n_dom)

    def column(first, last, act):
        @pl.loop(first, last)
        def _(part):
            for section in range(flow):
                act(section, part)

    partners = jnp.where(is_structure, flow * n_dom, known)
    for offset in neighbour_offsets:
        partners = partners + present(offset).astype(jnp.int32)

        @pl.when(present(offset))
        def _():
            pl.semaphore_signal(barrier, inc=1, device_id={"dom": dom + offset})

    @pl.when(is_structure)
    def _():
        def greet(section, part):
            pl.semaphore_signal(barrier, inc=1, device_id={"sec": section, "dom": part})

        column(chip + 2, n_dom, greet)

    @pl.when(jnp.logical_not(is_structure))
    def _():
        @pl.loop(0, n_dom)
        def _(owner):
            pl.semaphore_signal(barrier, inc=1, device_id={"sec": flow, "dom": owner})

    def meet():
        pl.semaphore_wait(barrier, partners)

        @pl.when(is_structure)
        def _():
            def greet(section, part):
                pl.semaphore_signal(surf_ready.at[dom], inc=1, device_id={"sec": section, "dom": part})

            column(0, jnp.minimum(chip + 2, n_dom), greet)

    def piece_tiles(index):
        start, end = index * block_slots, (index + 1) * block_slots
        return start, end, start // LANES, (end + LANES - 1) // LANES

    def halo_copy(sweep, index):
        _, _, first, last = piece_tiles(index)
        width = (last - first) * LANES
        return pltpu.make_async_remote_copy(
            src_ref=out_buf.at[sweep, pl.ds(0, NVAR), pl.ds(first * LANES, width)],
            dst_ref=halo_recv.at[sweep, index, pl.ds(0, NVAR), pl.ds(0, width)],
            send_sem=halo_send_sem.at[sweep, index],
            recv_sem=halo_recv_sem.at[sweep, index],
            device_id={"dom": dom + neighbour_offsets[index]},
        )

    sub = lax.broadcasted_iota(jnp.int32, (ROWS, LANES), 0)
    block_lane = sub * cap + lane % cap

    def pack(values):
        packed = jnp.zeros((ROWS, LANES), F32)
        for row in range(NLOAD):
            packed = jnp.where(lane_block == row, lane_gather(spread(values[row : row + 1]), block_lane), packed)
        return packed

    def unpack(rows):
        values = jnp.zeros((ROWS, LANES), F32)
        for part, row in enumerate(rows):
            values = jnp.where(lane_block == part, lane_gather(spread(row), block_lane), values)
        return values

    def split_highs(values, high):
        first = values.astype(BF16).astype(F32)
        second = values - first
        rows = []
        for at in range(highs):
            here = high == at
            rows += [jnp.where(here, first, 0.0), jnp.where(here, second, 0.0)]
        return jnp.concatenate(rows, axis=0).astype(BF16)

    def scatter(lhs, rhs):
        return lax.dot_general(lhs, rhs, (((1,), (1,)), ((), ())), preferred_element_type=F32)

    def live_mask(tile):
        limit = jnp.zeros((ROWS, LANES), jnp.int32)
        for part in range(per_tile):
            limit = jnp.where(lane_block == part, live_s[0, 0, tile * per_tile + part], limit)
        return (lane % cap) < limit

    def state_tiles():
        return [state_buf[:, at * LANES : (at + 1) * LANES] for at in range(tiles)]

    def prepare(sweep):
        own = state_tiles()
        for at in range(ghost_tiles):
            columns = slice(at * LANES, (at + 1) * LANES)
            out_buf[sweep, :, columns] = gather_tiles(own, *split_index(list_v[0, :, columns]))

    def map_rows(row, tile):
        return map_v[row * NVAR : (row + 1) * NVAR, 0, tile * LANES : (tile + 1) * LANES]

    def prepare_disp(sweep):
        own = state_tiles()
        for section in range(flow):
            for tile in range(surf_tiles):
                index = node_v[section, :, tile * LANES : (tile + 1) * LANES]
                packed = pack(gather_tiles(own, *split_index(index)))
                for part in range(per_tile):
                    disp_send[sweep, section * n_dom + tile * per_tile + part] = packed[part : part + 1]

    def prepare_loads(sweep):
        own = state_tiles()
        for tile in range(surf_tiles):
            index = cell_v[0, :, tile * LANES : (tile + 1) * LANES]
            values = gather_tiles(own, *split_index(index))
            loads = sum_rows([pad_rows(map_rows(row, tile) * values[:NVAR]) for row in range(NLOAD)])
            packed = pack(jnp.where(live_mask(tile), loads, 0.0))
            for part in range(per_tile):
                load_send[sweep, tile * per_tile + part] = packed[part : part + 1]

    def send_halo(sweep):
        for index in reversed(range(NBR)):

            @pl.when(present(neighbour_offsets[index]))
            def _():
                halo_copy(sweep, index).start()

    def send_disp(sweep):
        def send(section, part):
            pltpu.make_async_remote_copy(
                src_ref=disp_send.at[sweep, section * n_dom + part],
                dst_ref=disp_recv.at[sweep, dom],
                send_sem=surf_send_sem.at[sweep],
                recv_sem=disp_recv_sem.at[sweep],
                device_id={"sec": section, "dom": part},
            ).start()

        column(0, n_dom, send)

    def load_copy(sweep, owner):
        return pltpu.make_async_remote_copy(
            src_ref=load_send.at[sweep, owner],
            dst_ref=load_recv.at[sweep, sec * n_dom + dom],
            send_sem=surf_send_sem.at[sweep],
            recv_sem=load_recv_sem.at[sweep],
            device_id={"sec": flow, "dom": owner},
        )

    def send_loads(sweep, first, last):
        @pl.loop(first, last)
        def _(at):
            load_copy(sweep, first + last - 1 - at).start()

    def send_far_loads():
        @pl.loop(own_far, n_dom)
        def _(owner):
            pltpu.make_async_remote_copy(
                src_ref=load_send.at[0, owner],
                dst_ref=relay_recv.at[owner],
                send_sem=surf_send_sem.at[0],
                recv_sem=relay_recv_sem.at[owner],
                device_id={"dom": dom + REACH},
            ).start()

    def wait_relay(owner, sem):
        pltpu.make_async_copy(relay_recv.at[owner], relay_recv.at[owner], sem.at[owner]).wait()

    def send_late_loads():
        @pl.loop(known, n_dom)
        def _(at):
            owner = known + n_dom - 1 - at
            pl.semaphore_wait(surf_ready.at[owner], 1)

            @pl.when(owner < own_far)
            def _():
                load_copy(0, owner).start()

            @pl.when(owner >= passed_far)
            def _():
                wait_relay(owner, relay_recv_sem)
                pltpu.make_async_remote_copy(
                    src_ref=relay_recv.at[owner],
                    dst_ref=load_recv.at[0, sec * n_dom + dom - REACH],
                    send_sem=relay_send_sem.at[owner],
                    recv_sem=load_recv_sem.at[0],
                    device_id={"sec": flow, "dom": owner},
                ).start()

    bits = [(sub & (1 << bit)) != 0 for bit in range(3)]

    def by_diagonals(found):
        found = [pad_rows(value) for value in found] + [jnp.zeros((ROWS, LANES), F32)] * (ROWS - NVAR)
        for bit in range(3):
            found = [jnp.where(bits[bit], found[(at + (1 << bit)) % ROWS], found[at]) for at in range(ROWS)]
        return [found[(ROWS - shift) % ROWS] for shift in range(ROWS)]

    def turn(value, by):
        return pltpu.roll(value, (ROWS - by) % ROWS, 0)

    def apply_diagonals(diagonals, value):
        terms = [diagonals[shift] * value for shift in range(ROWS)]
        terms = [terms[shift] + turn(terms[shift + 4], 4) for shift in range(4)]
        return terms[0] + turn(terms[1], 1) + turn(terms[2] + turn(terms[3], 1), 2)

    low_row = lax.broadcasted_iota(jnp.int32, (LOW, LANES), 0).astype(F32).astype(BF16)
    ones, zeros = jnp.ones((LOW, LANES), BF16), jnp.zeros((LOW, LANES), BF16)

    def one_hot(cell):
        low = jnp.broadcast_to((cell & (LOW - 1)).astype(F32), (LOW, LANES)).astype(BF16)
        return jnp.where(low_row == low, ones, zeros)

    def build_faces():
        live = count_s[0, 0]
        entry = lax.broadcasted_iota(jnp.int32, (1, LANES), 1)

        @pl.loop(0, faces // (STEP * LANES))
        def _(at):
            for piece in range(STEP):
                group = at * STEP + piece
                part = pl.ds(pl.multiple_of(group * LANES, LANES), LANES)
                found = by_diagonals([block_v[0, 0, row, :, part].astype(F32) for row in range(NVAR)])
                for shift in range(ROWS):
                    diagonal[group, shift] = found[shift]
                cell = target_v[0, :, part]
                onehot[group] = one_hot(cell)
                target_high[group] = jnp.where(entry + group * LANES < live, cell // LOW, highs)

    def build_cells():
        for at in range(tiles):
            columns = slice(at * LANES, (at + 1) * LANES)
            right_rows[:, columns] = pad_rows(right_v[pl.ds(at, NVAR, stride=tiles), :])
            found = by_diagonals(
                [inverse_v[pl.ds(row * NVAR * tiles + at, NVAR, stride=tiles), :] for row in range(NVAR)]
            )
            for shift in range(ROWS):
                inverse_diagonal[at, shift] = found[shift]

    def build_surface():
        for section in range(flow):
            for tile in range(surf_tiles):
                columns = slice(tile * LANES, (tile + 1) * LANES)
                cell = node_v[section, :, columns]
                if section == 0:
                    cell = jnp.where(is_structure, cell, cell_v[0, :, columns])
                surf_hot[section * surf_tiles + tile] = one_hot(cell)
                surf_high[section * surf_tiles + tile] = cell // LOW

    def local_gather():
        own = state_tiles()

        @pl.loop(0, faces // CHUNK)
        def _(at):
            for piece in range(CHUNK // LANES):
                part = pl.ds(pl.multiple_of(at * CHUNK + piece * LANES, LANES), LANES)
                gath[:, part] = gather_tiles(own, *split_index(source_v[0, :, part]))

    def receive_halo(sweep):
        for index in range(NBR):

            @pl.when(present(-neighbour_offsets[index]))
            def _():
                halo_copy(sweep, index).wait_recv()

        for at in range(ghost_tiles):
            total = jnp.zeros((ROWS, LANES), F32)
            for index in range(NBR):
                start, end, first, last = piece_tiles(index)
                if first <= at < last:
                    inside = (lane + at * LANES >= start) & (lane + at * LANES < end)
                    part = halo_recv[sweep, index, :, (at - first) * LANES : (at - first + 1) * LANES]
                    total = jnp.where(inside, part, total)
            ghost_buf[:, at * LANES : (at + 1) * LANES] = total

    def face_pass():
        halo = [ghost_buf[:, at * LANES : (at + 1) * LANES] for at in range(ghost_tiles)]

        def step(at, total):
            lhs, rhs = [], []
            for piece in range(CHUNK // LANES):
                group = at * (CHUNK // LANES) + piece
                part = pl.ds(pl.multiple_of(group * LANES, LANES), LANES)
                high, low = split_index(source_v[0, :, part])
                high = high - tiles
                value = jnp.where(high >= 0, gather_tiles(halo, high, low), gath[:, part])
                contrib = apply_diagonals([diagonal[group, shift] for shift in range(ROWS)], value)
                lhs.append(split_highs(contrib, spread(target_high[group])))
                rhs.append(onehot[group])
            return total + scatter(jnp.concatenate(lhs, axis=1), jnp.concatenate(rhs, axis=1))

        return lax.fori_loop(0, faces // CHUNK, step, jnp.zeros((2 * ROWS * highs, LOW), F32))

    def surface_pass(sweep):
        @pl.when(is_structure)
        def _():
            pltpu.make_async_copy(load_recv.at[sweep], load_recv.at[sweep], load_recv_sem.at[sweep]).wait()
            lhs, rhs = [], []
            for section in range(flow):
                for tile in range(surf_tiles):
                    first = section * n_dom + tile * per_tile
                    at = section * surf_tiles + tile
                    values = unpack([load_recv[sweep, first + part] for part in range(per_tile)])
                    lhs.append(split_highs(values, spread(surf_high[at])))
                    rhs.append(surf_hot[at])
            surf_total[...] = scatter(jnp.concatenate(lhs, axis=1), jnp.concatenate(rhs, axis=1))

        @pl.when(jnp.logical_not(is_structure))
        def _():
            pltpu.make_async_copy(disp_recv.at[sweep], disp_recv.at[sweep], disp_recv_sem.at[sweep]).wait()
            lhs, rhs = [], []
            for tile in range(surf_tiles):
                back = unpack([disp_recv[sweep, tile * per_tile + part] for part in range(per_tile)])
                back = jnp.where(live_mask(tile), back, 0.0)
                pushed = map_rows(0, tile) * back[0:1]
                for row in range(1, NLOAD):
                    pushed = pushed + map_rows(row, tile) * back[row : row + 1]
                lhs.append(split_highs(pad_rows(pushed), spread(surf_high[tile])))
                rhs.append(surf_hot[tile])
            surf_total[...] = scatter(jnp.concatenate(lhs, axis=1), jnp.concatenate(rhs, axis=1))

    @pl.when(last)
    def _():
        meet()

    fetches[0].wait()
    for at in range(tiles):
        state_buf[:, at * LANES : (at + 1) * LANES] = pad_rows(init_v[pl.ds(at, NVAR, stride=tiles), :])
    fetches[1].wait()
    prepare(0)
    for fetch in fetches[2:6]:
        fetch.wait()

    @pl.when(is_structure)
    def _():
        prepare_disp(0)

    @pl.when(jnp.logical_not(is_structure))
    def _():
        prepare_loads(0)

    @pl.when(jnp.logical_not(last))
    def _():
        meet()

    @pl.when(is_structure)
    def _():
        send_disp(0)

    send_halo(0)

    @pl.when(jnp.logical_not(is_structure))
    def _():
        send_loads(0, 0, known)
        send_far_loads()

    build_surface()
    for fetch in fetches[6:8]:
        fetch.wait()
    build_faces()
    for fetch in fetches[8:]:
        fetch.wait()
    build_cells()
    local_gather()

    @pl.when(jnp.logical_not(is_structure))
    def _():
        send_late_loads()

    for sweep in range(ITERS):
        if sweep > 0:

            @pl.when(is_structure)
            def _():
                prepare_disp(sweep)
                send_disp(sweep)

            prepare(sweep)
            send_halo(sweep)

            @pl.when(jnp.logical_not(is_structure))
            def _():
                prepare_loads(sweep)
                send_loads(sweep, 0, n_dom)

            local_gather()
        receive_halo(sweep)
        total = face_pass()
        surface_pass(sweep)
        total = total + surf_total[...]
        for at in range(tiles):
            base = 2 * ROWS * (at * LANES // LOW)
            columns = slice(at * LANES % LOW, at * LANES % LOW + LANES)
            gone = total[base : base + ROWS, columns] + total[base + ROWS : base + 2 * ROWS, columns]
            rest = right_rows[:, at * LANES : (at + 1) * LANES] - gone
            fresh = apply_diagonals([inverse_diagonal[at, shift] for shift in range(ROWS)], rest)
            if sweep == ITERS - 1:
                out_ref[pl.ds(at, NVAR, stride=tiles), :] = fresh[:NVAR]
            else:
                state_buf[:, at * LANES : (at + 1) * LANES] = fresh

    for sweep in range(ITERS):
        for index in range(NBR):

            @pl.when(present(neighbour_offsets[index]))
            def _():
                halo_copy(sweep, index).wait_send()

        @pl.when(is_structure)
        def _():
            pltpu.make_async_copy(load_recv.at[sweep], load_recv.at[sweep], surf_send_sem.at[sweep]).wait()

        @pl.when(jnp.logical_not(is_structure))
        def _():
            pltpu.make_async_copy(disp_recv.at[sweep], disp_recv.at[sweep], surf_send_sem.at[sweep]).wait()

    @pl.when(jnp.logical_not(is_structure))
    def _():
        @pl.loop(passed_far, n_dom)
        def _(owner):
            wait_relay(owner, relay_send_sem)


def body(n_sec, n_dom, *args):
    cells = args[0].shape[-1]
    faces = args[4].shape[-1]
    ghosts = args[7].shape[-1]
    slots = args[8].shape[-1]
    flow = n_sec - 1
    piece = (2 * LANES - 1 + ghosts // NBR) // LANES * LANES
    args = list(args)
    for at in (0, 1, 2):
        args[at] = args[at].reshape(-1, LANES)
    args[10] = args[10].reshape(NLOAD * NVAR, 1, slots)
    fetched = [pltpu.VMEM(value.shape, value.dtype) for value in args]
    fetched[9] = pltpu.SMEM(args[9].shape, args[9].dtype)
    del fetched[6]
    groups = faces // LANES
    flat_rows = args[0].shape
    args = [value if at == 6 else pltpu.with_memory_space_constraint(value, pltpu.HBM) for at, value in enumerate(args)]
    specs = [pl.BlockSpec(memory_space=pltpu.HBM)] * len(args)
    specs[6] = pl.BlockSpec(memory_space=pltpu.SMEM)
    out = pl.pallas_call(
        functools.partial(kernel, (n_sec, n_dom, cells, faces, slots, ghosts)),
        out_shape=pltpu.VMEM(flat_rows, F32),
        in_specs=specs,
        out_specs=pl.BlockSpec(memory_space=pltpu.VMEM),
        scratch_shapes=[
            *fetched,
            pltpu.VMEM((ROWS, cells), F32),
            pltpu.VMEM((ITERS, ROWS, ghosts), F32),
            pltpu.VMEM((ITERS, NBR, ROWS, piece), F32),
            pltpu.VMEM((ROWS, ghosts), F32),
            pltpu.VMEM((ROWS, faces), F32),
            pltpu.VMEM((groups, ROWS, ROWS, LANES), F32),
            pltpu.VMEM((cells // LANES, ROWS, ROWS, LANES), F32),
            pltpu.VMEM((ROWS, cells), F32),
            pltpu.VMEM((groups, LOW, LANES), BF16),
            pltpu.VMEM((groups, 1, LANES), jnp.int32),
            pltpu.VMEM((flow * slots // LANES, LOW, LANES), BF16),
            pltpu.VMEM((flow * slots // LANES, 1, LANES), jnp.int32),
            pltpu.VMEM((2 * ROWS * (cells // LOW), LOW), F32),
            pltpu.VMEM((ITERS, n_dom, 1, LANES), F32),
            pltpu.VMEM((ITERS, flow * n_dom, 1, LANES), F32),
            pltpu.VMEM((n_dom, 1, LANES), F32),
            pltpu.VMEM((ITERS, flow * n_dom, 1, LANES), F32),
            pltpu.VMEM((ITERS, n_dom, 1, LANES), F32),
            pltpu.SemaphoreType.DMA((ITERS, NBR)),
            pltpu.SemaphoreType.DMA((ITERS, NBR)),
            pltpu.SemaphoreType.DMA((ITERS,)),
            pltpu.SemaphoreType.DMA((ITERS,)),
            pltpu.SemaphoreType.DMA((ITERS,)),
            pltpu.SemaphoreType.DMA((len(fetched),)),
            pltpu.SemaphoreType.DMA((n_dom,)),
            pltpu.SemaphoreType.DMA((n_dom,)),
            pltpu.SemaphoreType.REGULAR((n_dom,)),
        ],
        compiler_params=pltpu.CompilerParams(
            collective_id=0, has_side_effects=True, vmem_limit_bytes=48 * 1024 * 1024
        ),
    )(*args)
    return out.reshape(1, 1, NVAR, cells)


def solution(mesh):
    in_specs = (
        P("sec", "dom", None, None),
        P("sec", "dom", None, None),
        P("sec", "dom", None, None, None),
        P("sec", "dom", None, None, None),
        P("sec", "dom", None),
        P("sec", "dom", None),
        P("sec", "dom"),
        P("sec", "dom", None),
        P("sec", "dom", None),
        P("sec", "dom", None),
        P("sec", "dom", None, None, None),
        P(None, "dom", None),
    )
    out_specs = P("sec", "dom", None, None)
    run = functools.partial(body, mesh.shape["sec"], mesh.shape["dom"])
    return jax.shard_map(run, mesh=mesh, in_specs=in_specs, out_specs=out_specs, check_vma=False)
```

```python
import functools

import jax
import jax.numpy as jnp
from jax import lax
from jax.experimental import pallas as pl
from jax.experimental.pallas import tpu as pltpu
from jax.sharding import PartitionSpec as P

NVAR = 6
NLOAD = 3
NBR = 8
ITERS = 2
LANES = 128
LANE_BITS = 7
ROWS = 8
LOW = 128
CHUNK = 4608
STEP = 8
REACH = 4
FAR = 4

neighbour_offsets = (1, -1, 2, -2, 3, -3, 4, -4)

F32 = jnp.float32
BF16 = jnp.bfloat16


def lane_gather(table, index):
    return jnp.take_along_axis(table, index, axis=1, mode="promise_in_bounds")


def spread(row):
    return jnp.broadcast_to(row, (ROWS, row.shape[-1]))


def gather_tiles(tiles, high, low):
    found = [lane_gather(tile, low) for tile in tiles]
    bit = 1
    while len(found) > 1:
        odd = (high & bit) != 0
        pairs = [found[at : at + 2] for at in range(0, len(found), 2)]
        found = [jnp.where(odd, pair[1], pair[0]) if len(pair) == 2 else pair[0] for pair in pairs]
        bit *= 2
    return found[0]


def split_index(index):
    index = spread(index)
    return index >> LANE_BITS, index & (LANES - 1)


def sum_rows(parts):
    width = parts[0].shape[1]
    row = lax.broadcasted_iota(jnp.int32, (ROWS, width), 0)
    parts = list(parts) + [None] * (ROWS - len(parts))
    step = ROWS // 2
    while step >= 1:
        upper = (row & step) == 0
        merged = []
        for at in range(step):
            a, b = parts[at], parts[at + step]
            if a is None and b is None:
                merged.append(None)
                continue
            if b is None:
                kept, moved = jnp.where(upper, a, 0.0), jnp.where(upper, 0.0, a)
            else:
                kept, moved = jnp.where(upper, a, b), jnp.where(upper, b, a)
            if step == ROWS // 2:
                moved = pltpu.roll(moved, step, 0)
            else:
                moved = jnp.where(upper, pltpu.roll(moved, ROWS - step, 0), pltpu.roll(moved, step, 0))
            merged.append(kept + moved)
        parts = merged
        step //= 2
    return parts[0]


def pad_rows(value):
    return jnp.concatenate([value, jnp.zeros((ROWS - value.shape[0], value.shape[1]), value.dtype)], axis=0)


def kernel(
    dims,
    state_init,
    right_side,
    inverse,
    face_block,
    face_target,
    face_source,
    count_s,
    send_list,
    surf_cell,
    surf_count,
    surf_map,
    surf_node,
    out_ref,
    init_v,
    right_v,
    inverse_v,
    block_v,
    target_v,
    source_v,
    list_v,
    cell_v,
    live_s,
    map_v,
    node_v,
    state_buf,
    out_buf,
    halo_recv,
    ghost_buf,
    gath,
    diagonal,
    inverse_diagonal,
    right_rows,
    onehot,
    target_high,
    surf_hot,
    surf_high,
    surf_total,
    load_send,
    load_recv,
    relay_recv,
    disp_send,
    disp_recv,
    halo_send_sem,
    halo_recv_sem,
    surf_send_sem,
    load_recv_sem,
    disp_recv_sem,
    fetch_sem,
    relay_send_sem,
    relay_recv_sem,
    surf_ready,
):
    n_sec, n_dom, cells, faces, slots, ghosts = dims
    flow = n_sec - 1
    tiles = cells // LANES
    ghost_tiles = ghosts // LANES
    block_slots = ghosts // NBR
    surf_tiles = slots // LANES
    cap = slots // n_dom
    per_tile = LANES // cap
    highs = cells // LOW
    sec = lax.axis_index("sec")
    dom = lax.axis_index("dom")
    is_structure = sec == flow
    lane = lax.broadcasted_iota(jnp.int32, (ROWS, LANES), 1)
    lane_block = lane // cap

    def present(offset):
        target = dom + offset
        return (target >= 0) & (target < n_dom)

    order = (
        (state_init, init_v),
        (send_list, list_v),
        (surf_node, node_v),
        (surf_cell, cell_v),
        (surf_map, map_v),
        (surf_count, live_s),
        (face_block, block_v),
        (face_target, target_v),
        (face_source, source_v),
        (right_side, right_v),
        (inverse, inverse_v),
    )
    fetches = [pltpu.make_async_copy(src, dst, fetch_sem.at[at]) for at, (src, dst) in enumerate(order)]
    for fetch in fetches:
        fetch.start()

    halo_recv[...] = jnp.zeros(halo_recv.shape, F32)

    barrier = pltpu.get_barrier_semaphore()
    chip = dom // 2 * 2
    known = jnp.minimum(chip, n_dom)
    last = is_structure & (dom >= n_dom - 2)

    def far_owners(part):
        return jnp.minimum(part // 2 * 2 + FAR, n_dom)

    own_far = far_owners(dom)
    passed_far = jnp.where(dom >= REACH, far_owners(dom - REACH), n_dom)

    def column(first, last, act):
        @pl.loop(first, last)
        def _(part):
            for section in range(flow):
                act(section, part)

    partners = jnp.where(is_structure, flow * n_dom, known)
    for offset in neighbour_offsets:
        partners = partners + present(offset).astype(jnp.int32)

        @pl.when(present(offset))
        def _():
            pl.semaphore_signal(barrier, inc=1, device_id={"dom": dom + offset})

    @pl.when(is_structure)
    def _():
        def greet(section, part):
            pl.semaphore_signal(barrier, inc=1, device_id={"sec": section, "dom": part})

        column(chip + 2, n_dom, greet)

    @pl.when(jnp.logical_not(is_structure))
    def _():
        @pl.loop(0, n_dom)
        def _(owner):
            pl.semaphore_signal(barrier, inc=1, device_id={"sec": flow, "dom": owner})

    def meet():
        pl.semaphore_wait(barrier, partners)

        @pl.when(is_structure)
        def _():
            def greet(section, part):
                pl.semaphore_signal(surf_ready.at[dom], inc=1, device_id={"sec": section, "dom": part})

            column(0, jnp.minimum(chip + 2, n_dom), greet)

    def piece_tiles(index):
        start, end = index * block_slots, (index + 1) * block_slots
        return start, end, start // LANES, (end + LANES - 1) // LANES

    def halo_copy(sweep, index):
        _, _, first, last = piece_tiles(index)
        width = (last - first) * LANES
        return pltpu.make_async_remote_copy(
            src_ref=out_buf.at[sweep, pl.ds(0, NVAR), pl.ds(first * LANES, width)],
            dst_ref=halo_recv.at[sweep, index, pl.ds(0, NVAR), pl.ds(0, width)],
            send_sem=halo_send_sem.at[sweep, index],
            recv_sem=halo_recv_sem.at[sweep, index],
            device_id={"dom": dom + neighbour_offsets[index]},
        )

    sub = lax.broadcasted_iota(jnp.int32, (ROWS, LANES), 0)
    block_lane = sub * cap + lane % cap

    def pack(values):
        packed = jnp.zeros((ROWS, LANES), F32)
        for row in range(NLOAD):
            packed = jnp.where(lane_block == row, lane_gather(spread(values[row : row + 1]), block_lane), packed)
        return packed

    def unpack(rows):
        values = jnp.zeros((ROWS, LANES), F32)
        for part, row in enumerate(rows):
            values = jnp.where(lane_block == part, lane_gather(spread(row), block_lane), values)
        return values

    def split_highs(values, high):
        first = values.astype(BF16).astype(F32)
        second = values - first
        rows = []
        for at in range(highs):
            here = high == at
            rows += [jnp.where(here, first, 0.0), jnp.where(here, second, 0.0)]
        return jnp.concatenate(rows, axis=0).astype(BF16)

    def scatter(lhs, rhs):
        return lax.dot_general(lhs, rhs, (((1,), (1,)), ((), ())), preferred_element_type=F32)

    def live_mask(tile):
        limit = jnp.zeros((ROWS, LANES), jnp.int32)
        for part in range(per_tile):
            limit = jnp.where(lane_block == part, live_s[0, 0, tile * per_tile + part], limit)
        return (lane % cap) < limit

    def state_tiles():
        return [state_buf[:, at * LANES : (at + 1) * LANES] for at in range(tiles)]

    def prepare(sweep, first=0, last=ghost_tiles):
        own = state_tiles()
        for at in range(first, last):
            columns = slice(at * LANES, (at + 1) * LANES)
            out_buf[sweep, :, columns] = gather_tiles(own, *split_index(list_v[0, :, columns]))

    def map_rows(row, tile):
        return map_v[row * NVAR : (row + 1) * NVAR, 0, tile * LANES : (tile + 1) * LANES]

    def prepare_disp(sweep):
        own = state_tiles()
        for section in range(flow):
            for tile in range(surf_tiles):
                index = node_v[section, :, tile * LANES : (tile + 1) * LANES]
                packed = pack(gather_tiles(own, *split_index(index)))
                for part in range(per_tile):
                    disp_send[sweep, section * n_dom + tile * per_tile + part] = packed[part : part + 1]

    def prepare_loads(sweep):
        own = state_tiles()
        for tile in range(surf_tiles):
            index = cell_v[0, :, tile * LANES : (tile + 1) * LANES]
            values = gather_tiles(own, *split_index(index))
            loads = sum_rows([pad_rows(map_rows(row, tile) * values[:NVAR]) for row in range(NLOAD)])
            packed = pack(jnp.where(live_mask(tile), loads, 0.0))
            for part in range(per_tile):
                load_send[sweep, tile * per_tile + part] = packed[part : part + 1]

    def send_halo(sweep, first=0, last=NBR):
        for index in reversed(range(first, last)):

            @pl.when(present(neighbour_offsets[index]))
            def _():
                halo_copy(sweep, index).start()

    def send_disp(sweep):
        def send(section, part):
            pltpu.make_async_remote_copy(
                src_ref=disp_send.at[sweep, section * n_dom + part],
                dst_ref=disp_recv.at[sweep, dom],
                send_sem=surf_send_sem.at[sweep],
                recv_sem=disp_recv_sem.at[sweep],
                device_id={"sec": section, "dom": part},
            ).start()

        column(0, n_dom, send)

    def load_copy(sweep, owner):
        return pltpu.make_async_remote_copy(
            src_ref=load_send.at[sweep, owner],
            dst_ref=load_recv.at[sweep, sec * n_dom + dom],
            send_sem=surf_send_sem.at[sweep],
            recv_sem=load_recv_sem.at[sweep],
            device_id={"sec": flow, "dom": owner},
        )

    def send_loads(sweep, first, last):
        @pl.loop(first, last)
        def _(at):
            load_copy(sweep, first + last - 1 - at).start()

    def send_far_loads():
        @pl.loop(own_far, n_dom)
        def _(owner):
            pltpu.make_async_remote_copy(
                src_ref=load_send.at[0, owner],
                dst_ref=relay_recv.at[owner],
                send_sem=surf_send_sem.at[0],
                recv_sem=relay_recv_sem.at[owner],
                device_id={"dom": dom + REACH},
            ).start()

    def wait_relay(owner, sem):
        pltpu.make_async_copy(relay_recv.at[owner], relay_recv.at[owner], sem.at[owner]).wait()

    def send_late_loads():
        @pl.loop(known, n_dom)
        def _(at):
            owner = known + n_dom - 1 - at
            pl.semaphore_wait(surf_ready.at[owner], 1)

            @pl.when(owner < own_far)
            def _():
                load_copy(0, owner).start()

            @pl.when(owner >= passed_far)
            def _():
                wait_relay(owner, relay_recv_sem)
                pltpu.make_async_remote_copy(
                    src_ref=relay_recv.at[owner],
                    dst_ref=load_recv.at[0, sec * n_dom + dom - REACH],
                    send_sem=relay_send_sem.at[owner],
                    recv_sem=load_recv_sem.at[0],
                    device_id={"sec": flow, "dom": owner},
                ).start()

    bits = [(sub & (1 << bit)) != 0 for bit in range(3)]

    def by_diagonals(found):
        found = [pad_rows(value) for value in found] + [jnp.zeros((ROWS, LANES), F32)] * (ROWS - NVAR)
        for bit in range(3):
            found = [jnp.where(bits[bit], found[(at + (1 << bit)) % ROWS], found[at]) for at in range(ROWS)]
        return [found[(ROWS - shift) % ROWS] for shift in range(ROWS)]

    def turn(value, by):
        return pltpu.roll(value, (ROWS - by) % ROWS, 0)

    def apply_diagonals(diagonals, value):
        terms = [diagonals[shift] * value for shift in range(ROWS)]
        terms = [terms[shift] + turn(terms[shift + 4], 4) for shift in range(4)]
        return terms[0] + turn(terms[1], 1) + turn(terms[2] + turn(terms[3], 1), 2)

    low_row = lax.broadcasted_iota(jnp.int32, (LOW, LANES), 0).astype(F32).astype(BF16)
    ones, zeros = jnp.ones((LOW, LANES), BF16), jnp.zeros((LOW, LANES), BF16)

    def one_hot(cell):
        low = jnp.broadcast_to((cell & (LOW - 1)).astype(F32), (LOW, LANES)).astype(BF16)
        return jnp.where(low_row == low, ones, zeros)

    def build_faces():
        live = count_s[0, 0]
        entry = lax.broadcasted_iota(jnp.int32, (1, LANES), 1)

        @pl.loop(0, faces // (STEP * LANES))
        def _(at):
            for piece in range(STEP):
                group = at * STEP + piece
                part = pl.ds(pl.multiple_of(group * LANES, LANES), LANES)
                found = by_diagonals([block_v[0, 0, row, :, part].astype(F32) for row in range(NVAR)])
                for shift in range(ROWS):
                    diagonal[group, shift] = found[shift]
                cell = target_v[0, :, part]
                onehot[group] = one_hot(cell)
                target_high[group] = jnp.where(entry + group * LANES < live, cell // LOW, highs)

    def build_cells():
        for at in range(tiles):
            columns = slice(at * LANES, (at + 1) * LANES)
            right_rows[:, columns] = pad_rows(right_v[pl.ds(at, NVAR, stride=tiles), :])
            found = by_diagonals(
                [inverse_v[pl.ds(row * NVAR * tiles + at, NVAR, stride=tiles), :] for row in range(NVAR)]
            )
            for shift in range(ROWS):
                inverse_diagonal[at, shift] = found[shift]

    def build_surface():
        for section in range(flow):
            for tile in range(surf_tiles):
                columns = slice(tile * LANES, (tile + 1) * LANES)
                cell = node_v[section, :, columns]
                if section == 0:
                    cell = jnp.where(is_structure, cell, cell_v[0, :, columns])
                surf_hot[section * surf_tiles + tile] = one_hot(cell)
                surf_high[section * surf_tiles + tile] = cell // LOW

    def local_gather():
        own = state_tiles()

        @pl.loop(0, faces // CHUNK)
        def _(at):
            for piece in range(CHUNK // LANES):
                part = pl.ds(pl.multiple_of(at * CHUNK + piece * LANES, LANES), LANES)
                gath[:, part] = gather_tiles(own, *split_index(source_v[0, :, part]))

    def receive_halo(sweep):
        for index in range(NBR):

            @pl.when(present(-neighbour_offsets[index]))
            def _():
                halo_copy(sweep, index).wait_recv()

        for at in range(ghost_tiles):
            total = jnp.zeros((ROWS, LANES), F32)
            for index in range(NBR):
                start, end, first, last = piece_tiles(index)
                if first <= at < last:
                    inside = (lane + at * LANES >= start) & (lane + at * LANES < end)
                    part = halo_recv[sweep, index, :, (at - first) * LANES : (at - first + 1) * LANES]
                    total = jnp.where(inside, part, total)
            ghost_buf[:, at * LANES : (at + 1) * LANES] = total

    def face_pass():
        halo = [ghost_buf[:, at * LANES : (at + 1) * LANES] for at in range(ghost_tiles)]

        def step(at, total):
            lhs, rhs = [], []
            for piece in range(CHUNK // LANES):
                group = at * (CHUNK // LANES) + piece
                part = pl.ds(pl.multiple_of(group * LANES, LANES), LANES)
                high, low = split_index(source_v[0, :, part])
                high = high - tiles
                value = jnp.where(high >= 0, gather_tiles(halo, high, low), gath[:, part])
                contrib = apply_diagonals([diagonal[group, shift] for shift in range(ROWS)], value)
                lhs.append(split_highs(contrib, spread(target_high[group])))
                rhs.append(onehot[group])
            return total + scatter(jnp.concatenate(lhs, axis=1), jnp.concatenate(rhs, axis=1))

        return lax.fori_loop(0, faces // CHUNK, step, jnp.zeros((2 * ROWS * highs, LOW), F32))

    def surface_pass(sweep):
        @pl.when(is_structure)
        def _():
            pltpu.make_async_copy(load_recv.at[sweep], load_recv.at[sweep], load_recv_sem.at[sweep]).wait()
            lhs, rhs = [], []
            for section in range(flow):
                for tile in range(surf_tiles):
                    first = section * n_dom + tile * per_tile
                    at = section * surf_tiles + tile
                    values = unpack([load_recv[sweep, first + part] for part in range(per_tile)])
                    lhs.append(split_highs(values, spread(surf_high[at])))
                    rhs.append(surf_hot[at])
            surf_total[...] = scatter(jnp.concatenate(lhs, axis=1), jnp.concatenate(rhs, axis=1))

        @pl.when(jnp.logical_not(is_structure))
        def _():
            pltpu.make_async_copy(disp_recv.at[sweep], disp_recv.at[sweep], disp_recv_sem.at[sweep]).wait()
            lhs, rhs = [], []
            for tile in range(surf_tiles):
                back = unpack([disp_recv[sweep, tile * per_tile + part] for part in range(per_tile)])
                back = jnp.where(live_mask(tile), back, 0.0)
                pushed = map_rows(0, tile) * back[0:1]
                for row in range(1, NLOAD):
                    pushed = pushed + map_rows(row, tile) * back[row : row + 1]
                lhs.append(split_highs(pad_rows(pushed), spread(surf_high[tile])))
                rhs.append(surf_hot[tile])
            surf_total[...] = scatter(jnp.concatenate(lhs, axis=1), jnp.concatenate(rhs, axis=1))

    @pl.when(last)
    def _():
        meet()

    fetches[0].wait()
    for at in range(tiles):
        state_buf[:, at * LANES : (at + 1) * LANES] = pad_rows(init_v[pl.ds(at, NVAR, stride=tiles), :])
    fetches[1].wait()
    prepare(0)
    for fetch in fetches[2:6]:
        fetch.wait()

    @pl.when(is_structure)
    def _():
        prepare_disp(0)

    @pl.when(jnp.logical_not(is_structure))
    def _():
        prepare_loads(0)

    @pl.when(jnp.logical_not(last))
    def _():
        meet()

    @pl.when(is_structure)
    def _():
        send_disp(0)

    send_halo(0)

    @pl.when(jnp.logical_not(is_structure))
    def _():
        send_loads(0, 0, known)
        send_far_loads()

    build_surface()
    for fetch in fetches[6:8]:
        fetch.wait()
    build_faces()
    for fetch in fetches[8:]:
        fetch.wait()
    build_cells()
    local_gather()

    @pl.when(jnp.logical_not(is_structure))
    def _():
        send_late_loads()

    for sweep in range(ITERS):
        if sweep > 0:

            @pl.when(is_structure)
            def _():
                prepare_disp(sweep)
                send_disp(sweep)

            middle = piece_tiles(NBR // 2)[2]
            prepare(sweep, middle, ghost_tiles)
            send_halo(sweep, NBR // 2, NBR)
            prepare(sweep, 0, piece_tiles(NBR // 2 - 1)[3])
            send_halo(sweep, 0, NBR // 2)

            @pl.when(jnp.logical_not(is_structure))
            def _():
                prepare_loads(sweep)
                send_loads(sweep, 0, n_dom)

            local_gather()
        receive_halo(sweep)
        total = face_pass()
        surface_pass(sweep)
        total = total + surf_total[...]
        for at in range(tiles):
            base = 2 * ROWS * (at * LANES // LOW)
            columns = slice(at * LANES % LOW, at * LANES % LOW + LANES)
            gone = total[base : base + ROWS, columns] + total[base + ROWS : base + 2 * ROWS, columns]
            rest = right_rows[:, at * LANES : (at + 1) * LANES] - gone
            fresh = apply_diagonals([inverse_diagonal[at, shift] for shift in range(ROWS)], rest)
            if sweep == ITERS - 1:
                out_ref[pl.ds(at, NVAR, stride=tiles), :] = fresh[:NVAR]
            else:
                state_buf[:, at * LANES : (at + 1) * LANES] = fresh

    for sweep in range(ITERS):
        for index in range(NBR):

            @pl.when(present(neighbour_offsets[index]))
            def _():
                halo_copy(sweep, index).wait_send()

        @pl.when(is_structure)
        def _():
            pltpu.make_async_copy(load_recv.at[sweep], load_recv.at[sweep], surf_send_sem.at[sweep]).wait()

        @pl.when(jnp.logical_not(is_structure))
        def _():
            pltpu.make_async_copy(disp_recv.at[sweep], disp_recv.at[sweep], surf_send_sem.at[sweep]).wait()

    @pl.when(jnp.logical_not(is_structure))
    def _():
        @pl.loop(passed_far, n_dom)
        def _(owner):
            wait_relay(owner, relay_send_sem)


def body(n_sec, n_dom, *args):
    cells = args[0].shape[-1]
    faces = args[4].shape[-1]
    ghosts = args[7].shape[-1]
    slots = args[8].shape[-1]
    flow = n_sec - 1
    piece = (2 * LANES - 1 + ghosts // NBR) // LANES * LANES
    args = list(args)
    for at in (0, 1, 2):
        args[at] = args[at].reshape(-1, LANES)
    args[10] = args[10].reshape(NLOAD * NVAR, 1, slots)
    fetched = [pltpu.VMEM(value.shape, value.dtype) for value in args]
    fetched[9] = pltpu.SMEM(args[9].shape, args[9].dtype)
    del fetched[6]
    groups = faces // LANES
    flat_rows = args[0].shape
    args = [value if at == 6 else pltpu.with_memory_space_constraint(value, pltpu.HBM) for at, value in enumerate(args)]
    specs = [pl.BlockSpec(memory_space=pltpu.HBM)] * len(args)
    specs[6] = pl.BlockSpec(memory_space=pltpu.SMEM)
    out = pl.pallas_call(
        functools.partial(kernel, (n_sec, n_dom, cells, faces, slots, ghosts)),
        out_shape=pltpu.VMEM(flat_rows, F32),
        in_specs=specs,
        out_specs=pl.BlockSpec(memory_space=pltpu.VMEM),
        scratch_shapes=[
            *fetched,
            pltpu.VMEM((ROWS, cells), F32),
            pltpu.VMEM((ITERS, ROWS, ghosts), F32),
            pltpu.VMEM((ITERS, NBR, ROWS, piece), F32),
            pltpu.VMEM((ROWS, ghosts), F32),
            pltpu.VMEM((ROWS, faces), F32),
            pltpu.VMEM((groups, ROWS, ROWS, LANES), F32),
            pltpu.VMEM((cells // LANES, ROWS, ROWS, LANES), F32),
            pltpu.VMEM((ROWS, cells), F32),
            pltpu.VMEM((groups, LOW, LANES), BF16),
            pltpu.VMEM((groups, 1, LANES), jnp.int32),
            pltpu.VMEM((flow * slots // LANES, LOW, LANES), BF16),
            pltpu.VMEM((flow * slots // LANES, 1, LANES), jnp.int32),
            pltpu.VMEM((2 * ROWS * (cells // LOW), LOW), F32),
            pltpu.VMEM((ITERS, n_dom, 1, LANES), F32),
            pltpu.VMEM((ITERS, flow * n_dom, 1, LANES), F32),
            pltpu.VMEM((n_dom, 1, LANES), F32),
            pltpu.VMEM((ITERS, flow * n_dom, 1, LANES), F32),
            pltpu.VMEM((ITERS, n_dom, 1, LANES), F32),
            pltpu.SemaphoreType.DMA((ITERS, NBR)),
            pltpu.SemaphoreType.DMA((ITERS, NBR)),
            pltpu.SemaphoreType.DMA((ITERS,)),
            pltpu.SemaphoreType.DMA((ITERS,)),
            pltpu.SemaphoreType.DMA((ITERS,)),
            pltpu.SemaphoreType.DMA((len(fetched),)),
            pltpu.SemaphoreType.DMA((n_dom,)),
            pltpu.SemaphoreType.DMA((n_dom,)),
            pltpu.SemaphoreType.REGULAR((n_dom,)),
        ],
        compiler_params=pltpu.CompilerParams(
            collective_id=0, has_side_effects=True, vmem_limit_bytes=48 * 1024 * 1024
        ),
    )(*args)
    return out.reshape(1, 1, NVAR, cells)


def solution(mesh):
    in_specs = (
        P("sec", "dom", None, None),
        P("sec", "dom", None, None),
        P("sec", "dom", None, None, None),
        P("sec", "dom", None, None, None),
        P("sec", "dom", None),
        P("sec", "dom", None),
        P("sec", "dom"),
        P("sec", "dom", None),
        P("sec", "dom", None),
        P("sec", "dom", None),
        P("sec", "dom", None, None, None),
        P(None, "dom", None),
    )
    out_specs = P("sec", "dom", None, None)
    run = functools.partial(body, mesh.shape["sec"], mesh.shape["dom"])
    return jax.shard_map(run, mesh=mesh, in_specs=in_specs, out_specs=out_specs, check_vma=False)
```
